32 devices in a mesh: panel: 2 (over y), dom: 4 (over z), blk: 2 (over x), dir: 2 (over core).
Axes of the slice: x: 2, y: 2, z: 4, core: 2. Of those that a mesh axis runs over, the one named last changes fastest.
Arguments:
- panel_vectors: bfloat16 [3072, 2048], P('dom', ('panel', 'blk')), parts along dimension 1, may hold values from -6 to 6
- force_blocks: float32 [16, 9, 1024], P(None, None, 'dom'), may hold values from -1 to 1
- bond_vectors: float32 [2, 16, 1024], P('dir', None, 'dom'), may hold values from -4 to 4
- neighbours: int32 [16, 1024], P(None, 'dom'), may hold values from 0 to 511
- boundary_low: int32 [512], P('dom'), may hold values from 0 to 255
- boundary_high: int32 [512], P('dom'), may hold values from 0 to 255
Outputs:
- coupling: float32 [2, 2048, 1024], P('dir', ('panel', 'dom'), 'blk'), parts along dimension 1
The draws below stay inside these ranges and needn't reach their ends.
There are 2 independent parts, one for each index of `panel`. The reference program is written for one: setup_inputs(seed, part) draws one part's arguments, and reference() takes and returns one part's arrays. A program takes and returns all parts, laid end to end along the dimension named above; an argument that names none is the same for every part. Nothing has to cross between parts.
Inputs may be any that keep to these rules, and one draw needn't show every extreme that they name: `neighbours`: an entry below 256 names an atom of the same domain; from 256 to 383 the listed boundary atoms of the domain below; from 384 on those of the domain above. `boundary_low`: local atom numbers within the domain that owns the block; repeats may occur. `boundary_high`: local atom numbers within the domain that owns the block; repeats may occur.
All inputs are finite; a program needn't handle non-finite values.
Results may differ from the reference program's by a relative error of at most 0.0029.
Values may be sent and summed in bfloat16 or wider, within the bound.
A program may use at most 64 MiB of HBM per device.

```python
import jax
import jax.numpy as jnp
from jax import lax

AD = 256
M = 1024
K = 16
BND = 128
ATOMS = 1024
N_DOM = 4


def set_ends(entries, stream_key, least, top_value):
    longest = entries.shape.index(max(entries.shape))
    spots = []
    for shift in (0, 1):
        where = [jax.random.randint(jax.random.fold_in(stream_key, axis), (), 0, length) for axis, length in enumerate(entries.shape)]
        where[longest] = (where[longest] + shift) % entries.shape[longest]
        spots.append(tuple(where))
    return entries.at[spots[0]].set(least).at[spots[1]].set(top_value)


def block_levels(rng, shape, shards, smallest, high):
    level = 1.0
    for position, blocks in shards:
        draws = jax.random.uniform(jax.random.fold_in(jax.random.fold_in(rng, 6), position), (blocks,), jnp.float32, smallest / len(shards), high / len(shards))
        level = level * jnp.repeat(jnp.exp(draws), shape[position] // blocks).reshape((-1,) + (1,) * (len(shape) - 1 - position))
    return level


def noise(key, extent, spread, reach, shards=(), kind=jnp.bfloat16):
    drawn = spread * jax.random.normal(key, extent, jnp.float32)
    if shards:
        drawn = drawn * block_levels(key, extent, shards, -0.22, 0.18)
    return jnp.clip(drawn, -reach, reach).astype(kind)


def setup_inputs(seed: int = 0, part: int = 0) -> dict:
    streams_of = jax.random.split(jax.random.key(seed), 7)
    own_keys = jax.random.split(jax.random.fold_in(streams_of[6], part), 7)
    return {
        "panel_vectors": noise(own_keys[0], (3 * ATOMS, M), 1.0, 6.0, ((0, 4), (1, 2))),
        "force_blocks": noise(streams_of[1], (K, 9, ATOMS), 0.15, 1.0, ((2, 4),), jnp.float32),
        "bond_vectors": noise(streams_of[2], (2, K, ATOMS), 1.0, 4.0, ((0, 2), (2, 4)), jnp.float32),
        "neighbours": set_ends(jax.random.randint(streams_of[3], (K, ATOMS), 0, AD + 2 * BND), jax.random.fold_in(streams_of[3], 1), 0, (AD + 2 * BND) - 1).astype(jnp.int32),
        "boundary_low": set_ends(jax.random.randint(streams_of[4], (BND * N_DOM,), 0, AD), jax.random.fold_in(streams_of[4], 1), 0, AD - 1).astype(jnp.int32),
        "boundary_high": set_ends(jax.random.randint(streams_of[5], (BND * N_DOM,), 0, AD), jax.random.fold_in(streams_of[5], 1), 0, AD - 1).astype(jnp.int32),
    }


def flux_of(ext, forces, bond, nbrs):
    weights = forces * bond[:, None, :]
    atoms = nbrs.shape[1]

    def step(total, k):
        gathered = ext[nbrs[k]].astype(jnp.float32)
        blocks = weights[k].reshape(3, 3, atoms).transpose(2, 0, 1)
        return total + jnp.sum(blocks[:, :, :, None] * gathered[:, None, :, :], axis=2), None

    init = jnp.zeros((atoms, 3, ext.shape[2]), jnp.float32)
    total, unused = lax.scan(step, init, jnp.arange(K, dtype=jnp.int32))
    return total


def reference(panel_vectors, force_blocks, bond_vectors, neighbours, boundary_low, boundary_high):
    stacked = panel_vectors.reshape(N_DOM, AD, 3, M)

    def domain(d, coupling):
        prev = jnp.mod(d - 1 + N_DOM, N_DOM).astype(jnp.int32)
        nextd = jnp.mod(d + 1, N_DOM).astype(jnp.int32)
        own = lax.dynamic_slice_in_dim(stacked, d, 1, 0)[0]
        low_src = lax.dynamic_slice_in_dim(stacked, prev, 1, 0)[0]
        high_src = lax.dynamic_slice_in_dim(stacked, nextd, 1, 0)[0]
        upper_list = lax.dynamic_slice_in_dim(boundary_high, (prev * BND).astype(jnp.int32), BND, 0)
        lower_list = lax.dynamic_slice_in_dim(boundary_low, (nextd * BND).astype(jnp.int32), BND, 0)
        ext = jnp.concatenate([own, low_src[upper_list], high_src[lower_list]], axis=0)
        start = (d * AD).astype(jnp.int32)
        forces = lax.dynamic_slice_in_dim(force_blocks, start, AD, 2)
        bonds = lax.dynamic_slice_in_dim(bond_vectors, start, AD, 2)
        nbrs = lax.dynamic_slice_in_dim(neighbours, start, AD, 1)
        own_rows = own.reshape(3 * AD, M)
        parts = []
        for c in range(2):
            flux = flux_of(ext, forces, bonds[c], nbrs).astype(jnp.bfloat16).reshape(3 * AD, M)
            parts.append(jnp.dot(own_rows.T, flux, preferred_element_type=jnp.float32))
        return coupling + jnp.stack(parts, axis=0)

    coupling = lax.fori_loop(0, N_DOM, domain, jnp.zeros((2, M, M), jnp.float32))
    return coupling * ((3.0 * ATOMS) ** -0.5)
```

```python
import functools

import jax
import jax.numpy as jnp
from jax import lax
from jax.experimental import pallas as pl
from jax.experimental.pallas import tpu as pltpu
from jax.sharding import PartitionSpec as P

MESH = pl.DeviceIdType.MESH
BF16 = jnp.bfloat16
F32 = jnp.float32


def one_hot(hits):
    return jnp.where(hits, 1.0, 0.0).astype(BF16)


def dot(a, b):
    return jnp.dot(a, b, preferred_element_type=F32)


def kernel(n, nblk, pieces, v_ref, force_ref, bond_ref, nbr_ref, low_ref, high_ref, out_ref,
           vbuf, vt, vx, perm, hs, ht, fv, wq, bv, nv, lv, st_hi, st_lo, flux, part, su, ru, sd, rd,
           in_sem, h_send, h_recv, hf_send, hf_recv, x_send, x_recv, xf_send, xf_recv,
           u_send, u_recv, d_send, d_recv):
    me = lax.axis_index("dom")
    blk = lax.axis_index("blk")
    core = lax.axis_index("dir")
    rows, cols = v_ref.shape
    atoms = rows // 3
    half = cols // 2
    share = half // 2
    bnd = low_ref.shape[1]
    steps = nbr_ref.shape[0]
    tile = out_ref.shape[0]
    piece = tile // pieces
    up, down = lax.rem(me + 1, n), lax.rem(me + n - 1, n)

    fetches = [
        pltpu.make_async_copy(high_ref, lv.at[0], in_sem.at[0]),
        pltpu.make_async_copy(low_ref, lv.at[1], in_sem.at[1]),
        pltpu.make_async_copy(v_ref, vbuf, in_sem.at[2]),
        pltpu.make_async_copy(nbr_ref, nv, in_sem.at[3]),
        pltpu.make_async_copy(bond_ref.at[0], bv, in_sem.at[4]),
        pltpu.make_async_copy(force_ref, fv, in_sem.at[5]),
    ]
    barrier = pltpu.get_barrier_semaphore()
    peers = [{"dom": up}, {"dom": down}, {"dir": 1 - core}]
    peers += [{"blk": lax.rem(blk + o, nblk)} for o in range(1, nblk)]
    for peer in peers:
        pl.semaphore_signal(barrier, inc=1, device_id=peer, device_id_type=MESH)
    for copy in fetches:
        copy.start()

    row_of = lax.broadcasted_iota(jnp.int32, (rows, atoms), 0)
    atom_of = lax.broadcasted_iota(jnp.int32, (rows, atoms), 1)
    for a in range(3):
        perm[:, a * atoms:(a + 1) * atoms] = one_hot(row_of == 3 * atom_of + a)
    fetches[0].wait()
    fetches[1].wait()
    atom_row = lax.broadcasted_iota(jnp.int32, (atoms, bnd), 0)
    pick = jnp.concatenate([one_hot(atom_row == lv[side]) for side in range(2)], axis=1)

    fetches[2].wait()
    vt[...] = vbuf[...].T

    def own_rows(c):
        return [pl.ds(pl.multiple_of(h * half + c * share, share), share) for h in range(2)]

    def sort_rows(c):
        sorted_rows = dot(jnp.concatenate([vt[r, :] for r in own_rows(c)], axis=0), perm[...]).astype(BF16)
        for h in range(2):
            vx[blk, h, pl.ds(pl.multiple_of(c * share, share), share), :] = sorted_rows[h * share:(h + 1) * share]
        return sorted_rows

    mine = sort_rows(core)
    for b in range(3):
        rows_out = dot(mine[:, b * atoms:(b + 1) * atoms], pick).astype(BF16)
        for side in range(2):
            for h in range(2):
                hs[side, h, :, b * bnd:(b + 1) * bnd] = rows_out[
                    h * share:(h + 1) * share, side * bnd:(side + 1) * bnd]
    pl.semaphore_wait(barrier, len(peers))

    halo = {
        (side, h): pltpu.make_async_remote_copy(
            src_ref=hs.at[side, h], dst_ref=ht.at[side, h, core],
            send_sem=h_send.at[2 * side + h], recv_sem=h_recv.at[2 * side + h],
            device_id={"dom": up if side == 0 else down}, device_id_type=MESH)
        for h in range(2) for side in range(2)
    }
    for side in range(2):
        halo[side, 0].start()

    my_share = pl.ds(pl.multiple_of(core * share, share), share)

    def x_half(b, p):
        return lax.rem(b + p, 2)

    tiles = {
        (o, p): pltpu.make_async_remote_copy(
            src_ref=vx.at[blk, x_half(blk, p), my_share], dst_ref=vx.at[blk, x_half(blk, p), my_share],
            send_sem=x_send.at[2 * (o - 1) + p], recv_sem=x_recv.at[2 * (o - 1) + p],
            device_id={"blk": lax.rem(blk + o, nblk)}, device_id_type=MESH)
        for o in range(1, nblk) for p in range(2)
    }
    for o in range(1, nblk):
        tiles[o, 0].start()
    sort_rows(1 - core)

    for i in range(3, 6):
        fetches[i].wait()
    for q in range(9):
        wq[q] = fv[q] * bv[...]
    names = nv[...]
    k_of = lax.broadcasted_iota(jnp.int32, names.shape, 0)
    totals = [wq[q] for q in range(9)]
    for s in range(1, steps):
        same = (names == pltpu.roll(names, s, 0)) & (k_of >= s)
        for q in range(9):
            totals[q] = totals[q] + jnp.where(same, pltpu.roll(wq[q], s, 0), 0.0)
    for q in range(9):
        wq[q] = totals[q]

    sub, lanes, group = 8, 128, 32

    def build(first, count, base, stride):
        def body(t, carry):
            j0 = pl.multiple_of(t * group, group)
            for i0 in range(0, atoms, lanes):
                here = slice(i0, i0 + lanes)
                strips = range(group // sub)
                js = [lax.broadcasted_iota(jnp.int32, (sub, lanes), 0) + (j0 + first + s * sub) for s in strips]
                found = [jnp.full((sub, lanes), -1, jnp.int32) for _ in strips]
                for k in range(steps):
                    name = jnp.broadcast_to(nv[k:k + 1, here], (sub, lanes))
                    for s in strips:
                        found[s] = jnp.where(js[s] == name, k, found[s])
                spot = [f & (sub - 1) for f in found]
                for a in range(3):
                    for b in range(3):
                        values = []
                        for s in strips:
                            value = jnp.zeros((sub, lanes), F32)
                            for k0 in range(0, steps, sub):
                                taken = jnp.take_along_axis(
                                    wq[3 * a + b, k0:k0 + sub, here], spot[s], axis=0, mode="promise_in_bounds")
                                value = jnp.where(found[s] >= k0, taken, value)
                            values.append(value)
                        value = jnp.concatenate(values, axis=0)
                        high = value.astype(BF16)
                        at = (pl.ds(pl.multiple_of(base + b * stride + j0, group), group),
                              slice(a * atoms + i0, a * atoms + i0 + lanes))
                        st_hi[at] = high
                        st_lo[at] = (value - high.astype(F32)).astype(BF16)
            return carry

        lax.fori_loop(0, count // group, body, 0)

    build(0, atoms, 0, atoms)
    for o in range(1, nblk):
        tiles[o, 1].start()
    build(atoms, bnd, rows, bnd)
    for side in range(2):
        halo[side, 1].start()
    build(atoms + bnd, bnd, rows + 3 * bnd, bnd)

    onward = {}
    tiles_on = {}

    def pass_halo(h):
        for side in range(2):
            halo[side, h].wait_recv()
            onward[side, h] = pltpu.make_async_remote_copy(
                src_ref=ht.at[side, h, core], dst_ref=ht.at[side, h, core],
                send_sem=hf_send.at[2 * side + h], recv_sem=hf_recv.at[2 * side + h],
                device_id={"dir": 1 - core}, device_id_type=MESH)
            onward[side, h].start()

    def source(o):
        return lax.rem(blk + nblk - o, nblk)

    def pass_tiles(p):
        for o in range(1, nblk):
            tiles[o, p].wait_recv()
            spot = (source(o), x_half(source(o), p), my_share)
            tiles_on[o, p] = pltpu.make_async_remote_copy(
                src_ref=vx.at[spot], dst_ref=vx.at[spot],
                send_sem=xf_send.at[2 * (o - 1) + p], recv_sem=xf_recv.at[2 * (o - 1) + p],
                device_id={"dir": 1 - core}, device_id_type=MESH)
            tiles_on[o, p].start()

    def term(h, e, r):
        return part[h, pl.ds(pl.multiple_of(e * tile + r * piece, piece), piece), :]

    def hop(h, e, r, out, into, send, recv, target):
        cell = (h * n + e) * pieces + r
        here = pl.ds(r * piece, piece)
        return pltpu.make_async_remote_copy(
            src_ref=out.at[h, e, here], dst_ref=into.at[h, e, here],
            send_sem=send.at[cell], recv_sem=recv.at[cell],
            device_id={"dom": target}, device_id_type=MESH)

    def rising(h, e, r):
        return hop(h, e, r, su, ru, u_send, u_recv, up)

    def falling(h, e, r):
        return hop(h, e, r, sd, rd, d_send, d_recv, down)

    def ends(t):
        return ((me, n - 1 - (t - me), rising, su, ru),
                (n - 1 - me, t - (n - 1 - me), falling, sd, rd))

    def own_flux(h):
        own = vx[blk, h]
        flux[h] = dot(own, st_hi[:rows, :]) + dot(own, st_lo[:rows, :])

    def couple(h):
        for side in range(2):
            onward[side, h].wait_recv()
        outer = jnp.concatenate(
            [jnp.concatenate([ht[side, h, c] for side in range(2)], axis=1) for c in range(2)], axis=0)
        total = flux[h] + dot(outer, st_hi[rows:, :]) + dot(outer, st_lo[rows:, :])
        return total.astype(BF16).T

    def multiply(h, b, u, columns):
        part[h, pl.ds(pl.multiple_of((2 * b + u) * half, half), half), :] = dot(vx[b, u], columns)

    order = [(t, h) for h in range(2) for t in range(n - 1)]

    def emit(i):
        t, h = order[i]
        for way, (first, e, make, out, into) in enumerate(ends(t)):
            @pl.when(first == 0)
            def _(way=way, e=e, make=make, out=out):
                if i >= 2:
                    t_done, h_done = order[i - 2]
                    e_done = ends(t_done)[way][1]
                    for r in range(pieces):
                        make(h_done, e_done, r).wait_send()
                for r in range(pieces):
                    out[h, e, r * piece:(r + 1) * piece] = term(h, e, r).astype(out.dtype)
                    make(h, e, r).start()

    own_flux(0)
    pass_halo(0)
    own_flux(1)
    pass_tiles(0)
    columns = couple(0)
    for u in range(2):
        multiply(0, blk, u, columns)
    for o in range(1, nblk):
        tiles_on[o, 0].wait_recv()
        multiply(0, source(o), x_half(source(o), 0), columns)
    emit(0)
    pass_halo(1)
    later = couple(1)
    pass_tiles(1)
    for u in range(2):
        multiply(1, blk, u, later)
    for o in range(1, nblk):
        multiply(1, source(o), x_half(source(o), 0), later)
    for o in range(1, nblk):
        tiles_on[o, 1].wait_recv()
        multiply(0, source(o), x_half(source(o), 1), columns)
    emit(1)
    for o in range(1, nblk):
        multiply(1, source(o), x_half(source(o), 1), later)
    for i in range(2, len(order)):
        emit(i)

    for h in range(2):
        for t in range(1, n - 1):
            for r in range(pieces):
                for first, e, make, out, into in ends(t):
                    @pl.when((first > 0) & (first <= t))
                    def _(r=r, e=e, make=make, out=out, into=into):
                        here = slice(r * piece, (r + 1) * piece)
                        make(h, e, r).wait_recv()
                        out[h, e, here] = (term(h, e, r) + into[h, e, here].astype(F32)).astype(out.dtype)
                        make(h, e, r).start()

        for r in range(pieces):
            here = slice(r * piece, (r + 1) * piece)
            there = slice(h * half, (h + 1) * half)

            @pl.when(me == 0)
            def _():
                falling(h, me, r).wait_recv()
                out_ref[here, there] = term(h, me, r) + rd[h, me, here].astype(F32)

            @pl.when(me == n - 1)
            def _():
                rising(h, me, r).wait_recv()
                out_ref[here, there] = term(h, me, r) + ru[h, me, here].astype(F32)

            @pl.when((me > 0) & (me < n - 1))
            def _():
                rising(h, me, r).wait_recv()
                falling(h, me, r).wait_recv()
                out_ref[here, there] = (
                    term(h, me, r) + ru[h, me, here].astype(F32) + rd[h, me, here].astype(F32))

    for i, (t, h) in enumerate(order):
        for first, e, make, out, into in ends(t):
            early = i < len(order) - 2

            @pl.when((first <= t) & (first > 0) if early else first <= t)
            def _(e=e, make=make):
                for r in range(pieces):
                    make(h, e, r).wait_send()

    for copy in [*halo.values(), *onward.values(), *tiles.values(), *tiles_on.values()]:
        copy.wait_send()


def per_device(n, nblk, panel_vectors, force_blocks, bond_vectors, neighbours, boundary_low, boundary_high):
    rows, cols = panel_vectors.shape
    atoms = rows // 3
    half = cols // 2
    bnd = boundary_low.shape[0]
    steps = neighbours.shape[0]
    tile = nblk * cols // n
    wire = BF16 if n <= 4 else F32
    vmem = pl.BlockSpec(memory_space=pltpu.VMEM)
    hbm = pl.BlockSpec(memory_space=pltpu.HBM)
    pieces = 2
    line = pltpu.VMEM((2, n, tile, half), wire)
    hops = pltpu.SemaphoreType.DMA((2 * n * pieces,))
    dma = pltpu.SemaphoreType.DMA
    shares = dma((2 * (nblk - 1),))
    result = pl.pallas_call(
        functools.partial(kernel, n, nblk, pieces),
        out_shape=jax.ShapeDtypeStruct((tile, cols), F32),
        in_specs=[hbm] * 6,
        out_specs=vmem,
        scratch_shapes=[
            pltpu.VMEM((rows, cols), BF16),
            pltpu.VMEM((cols, rows), BF16),
            pltpu.VMEM((nblk, 2, half, rows), BF16),
            pltpu.VMEM((rows, rows), BF16),
            pltpu.VMEM((2, 2, half // 2, 3 * bnd), BF16),
            pltpu.VMEM((2, 2, 2, half // 2, 3 * bnd), BF16),
            pltpu.VMEM((9, steps, atoms), F32),
            pltpu.VMEM((9, steps, atoms), F32),
            pltpu.VMEM((steps, atoms), F32),
            pltpu.VMEM((steps, atoms), jnp.int32),
            pltpu.VMEM((2, 1, bnd), jnp.int32),
            pltpu.VMEM((rows + 6 * bnd, rows), BF16),
            pltpu.VMEM((rows + 6 * bnd, rows), BF16),
            pltpu.VMEM((2, half, rows), F32),
            pltpu.VMEM((2, nblk * cols, half), F32),
            line, line, line, line,
            dma((6,)), dma((4,)), dma((4,)), dma((4,)), dma((4,)),
            shares, shares, shares, shares,
            hops, hops, hops, hops,
        ],
        compiler_params=pltpu.CompilerParams(
            collective_id=0, has_side_effects=True, vmem_limit_bytes=60 * 1024 * 1024
        ),
    )(panel_vectors, jnp.transpose(force_blocks, (1, 0, 2)), bond_vectors, neighbours,
      boundary_low.reshape(1, bnd), boundary_high.reshape(1, bnd))
    scale = (3.0 * atoms * n) ** (-0.5)
    return (result * scale)[None, :, :]


def solution(mesh):
    in_specs = (
        P("dom", ("panel", "blk")),
        P(None, None, "dom"),
        P("dir", None, "dom"),
        P(None, "dom"),
        P("dom"),
        P("dom"),
    )
    out_specs = P("dir", ("panel", "dom"), "blk")
    return jax.shard_map(
        functools.partial(per_device, mesh.shape["dom"], mesh.shape["blk"]),
        mesh=mesh, in_specs=in_specs, out_specs=out_specs, check_vma=False
    )
```

```python
import functools

import jax
import jax.numpy as jnp
from jax import lax
from jax.experimental import pallas as pl
from jax.experimental.pallas import tpu as pltpu
from jax.sharding import PartitionSpec as P

MESH = pl.DeviceIdType.MESH
BF16 = jnp.bfloat16
F32 = jnp.float32


def one_hot(hits):
    return jnp.where(hits, 1.0, 0.0).astype(BF16)


def dot(a, b):
    return jnp.dot(a, b, preferred_element_type=F32)


def kernel(n, nblk, pieces, v_ref, force_ref, bond_ref, nbr_ref, low_ref, high_ref, out_ref,
           vbuf, vt, vx, perm, hs, ht, fv, wq, bv, nv, lv, st_hi, st_lo, flux, part, su, ru, sd, rd,
           in_sem, h_send, h_recv, hf_send, hf_recv, x_send, x_recv, xf_send, xf_recv,
           u_send, u_recv, d_send, d_recv):
    me = lax.axis_index("dom")
    blk = lax.axis_index("blk")
    core = lax.axis_index("dir")
    rows, cols = v_ref.shape
    atoms = rows // 3
    half = cols // 2
    share = half // 2
    bnd = low_ref.shape[1]
    steps = nbr_ref.shape[0]
    tile = out_ref.shape[0]
    piece = tile // pieces
    up, down = lax.rem(me + 1, n), lax.rem(me + n - 1, n)

    fetches = [
        pltpu.make_async_copy(high_ref, lv.at[0], in_sem.at[0]),
        pltpu.make_async_copy(low_ref, lv.at[1], in_sem.at[1]),
        pltpu.make_async_copy(v_ref, vbuf, in_sem.at[2]),
        pltpu.make_async_copy(nbr_ref, nv, in_sem.at[3]),
        pltpu.make_async_copy(bond_ref.at[0], bv, in_sem.at[4]),
        pltpu.make_async_copy(force_ref, fv, in_sem.at[5]),
    ]
    barrier = pltpu.get_barrier_semaphore()
    peers = [{"dom": up}, {"dom": down}, {"dir": 1 - core}]
    peers += [{"blk": lax.rem(blk + o, nblk)} for o in range(1, nblk)]
    for peer in peers:
        pl.semaphore_signal(barrier, inc=1, device_id=peer, device_id_type=MESH)
    for copy in fetches:
        copy.start()

    row_of = lax.broadcasted_iota(jnp.int32, (rows, atoms), 0)
    atom_of = lax.broadcasted_iota(jnp.int32, (rows, atoms), 1)
    for a in range(3):
        perm[:, a * atoms:(a + 1) * atoms] = one_hot(row_of == 3 * atom_of + a)
    fetches[0].wait()
    fetches[1].wait()
    atom_row = lax.broadcasted_iota(jnp.int32, (atoms, bnd), 0)
    pick = jnp.concatenate([one_hot(atom_row == lv[side]) for side in range(2)], axis=1)

    fetches[2].wait()
    vt[...] = vbuf[...].T

    def own_rows(c):
        return [pl.ds(pl.multiple_of(h * half + c * share, share), share) for h in range(2)]

    def sort_rows(c):
        sorted_rows = dot(jnp.concatenate([vt[r, :] for r in own_rows(c)], axis=0), perm[...]).astype(BF16)
        for h in range(2):
            vx[blk, h, pl.ds(pl.multiple_of(c * share, share), share), :] = sorted_rows[h * share:(h + 1) * share]
        return sorted_rows

    mine = sort_rows(core)
    for b in range(3):
        rows_out = dot(mine[:, b * atoms:(b + 1) * atoms], pick).astype(BF16)
        for side in range(2):
            for h in range(2):
                hs[side, h, :, b * bnd:(b + 1) * bnd] = rows_out[
                    h * share:(h + 1) * share, side * bnd:(side + 1) * bnd]
    pl.semaphore_wait(barrier, len(peers))

    halo = {
        (side, h): pltpu.make_async_remote_copy(
            src_ref=hs.at[side, h], dst_ref=ht.at[side, h, core],
            send_sem=h_send.at[2 * side + h], recv_sem=h_recv.at[2 * side + h],
            device_id={"dom": up if side == 0 else down}, device_id_type=MESH)
        for h in range(2) for side in range(2)
    }
    for side in range(2):
        halo[side, 0].start()

    my_share = pl.ds(pl.multiple_of(core * share, share), share)

    def x_half(b, p):
        return lax.rem(b + p, 2)

    tiles = {
        (o, p): pltpu.make_async_remote_copy(
            src_ref=vx.at[blk, x_half(blk, p), my_share], dst_ref=vx.at[blk, x_half(blk, p), my_share],
            send_sem=x_send.at[2 * (o - 1) + p], recv_sem=x_recv.at[2 * (o - 1) + p],
            device_id={"blk": lax.rem(blk + o, nblk)}, device_id_type=MESH)
        for o in range(1, nblk) for p in range(2)
    }
    for o in range(1, nblk):
        tiles[o, 0].start()
    sort_rows(1 - core)

    for i in range(3, 6):
        fetches[i].wait()
    for q in range(9):
        wq[q] = fv[q] * bv[...]
    names = nv[...]
    k_of = lax.broadcasted_iota(jnp.int32, names.shape, 0)
    totals = [wq[q] for q in range(9)]
    for s in range(1, steps):
        same = (names == pltpu.roll(names, s, 0)) & (k_of >= s)
        for q in range(9):
            totals[q] = totals[q] + jnp.where(same, pltpu.roll(wq[q], s, 0), 0.0)
    for q in range(9):
        wq[q] = totals[q]

    sub, lanes, group = 8, 128, 32

    def build(first, count, base, stride):
        def body(t, carry):
            j0 = pl.multiple_of(t * group, group)
            for i0 in range(0, atoms, lanes):
                here = slice(i0, i0 + lanes)
                strips = range(group // sub)
                js = [lax.broadcasted_iota(jnp.int32, (sub, lanes), 0) + (j0 + first + s * sub) for s in strips]
                found = [jnp.full((sub, lanes), -1, jnp.int32) for _ in strips]
                for k in range(steps):
                    name = jnp.broadcast_to(nv[k:k + 1, here], (sub, lanes))
                    for s in strips:
                        found[s] = jnp.where(js[s] == name, k, found[s])
                spot = [f & (sub - 1) for f in found]
                for a in range(3):
                    for b in range(3):
                        values = []
                        for s in strips:
                            value = jnp.zeros((sub, lanes), F32)
                            for k0 in range(0, steps, sub):
                                taken = jnp.take_along_axis(
                                    wq[3 * a + b, k0:k0 + sub, here], spot[s], axis=0, mode="promise_in_bounds")
                                value = jnp.where(found[s] >= k0, taken, value)
                            values.append(value)
                        value = jnp.concatenate(values, axis=0)
                        high = value.astype(BF16)
                        at = (pl.ds(pl.multiple_of(base + b * stride + j0, group), group),
                              slice(a * atoms + i0, a * atoms + i0 + lanes))
                        st_hi[at] = high
                        st_lo[at] = (value - high.astype(F32)).astype(BF16)
            return carry

        lax.fori_loop(0, count // group, body, 0)

    build(0, atoms, 0, atoms)
    for o in range(1, nblk):
        tiles[o, 1].start()
    build(atoms, bnd, rows, bnd)
    for side in range(2):
        halo[side, 1].start()
    build(atoms + bnd, bnd, rows + 3 * bnd, bnd)

    onward = {}
    tiles_on = {}

    def pass_halo(h):
        for side in range(2):
            halo[side, h].wait_recv()
            onward[side, h] = pltpu.make_async_remote_copy(
                src_ref=ht.at[side, h, core], dst_ref=ht.at[side, h, core],
                send_sem=hf_send.at[2 * side + h], recv_sem=hf_recv.at[2 * side + h],
                device_id={"dir": 1 - core}, device_id_type=MESH)
            onward[side, h].start()

    def source(o):
        return lax.rem(blk + nblk - o, nblk)

    def pass_tiles(p):
        for o in range(1, nblk):
            tiles[o, p].wait_recv()
            spot = (source(o), x_half(source(o), p), my_share)
            tiles_on[o, p] = pltpu.make_async_remote_copy(
                src_ref=vx.at[spot], dst_ref=vx.at[spot],
                send_sem=xf_send.at[2 * (o - 1) + p], recv_sem=xf_recv.at[2 * (o - 1) + p],
                device_id={"dir": 1 - core}, device_id_type=MESH)
            tiles_on[o, p].start()

    def term(h, e, r):
        return part[h, pl.ds(pl.multiple_of(e * tile + r * piece, piece), piece), :]

    def hop(h, e, r, out, into, send, recv, target):
        cell = (h * n + e) * pieces + r
        here = pl.ds(r * piece, piece)
        return pltpu.make_async_remote_copy(
            src_ref=out.at[h, e, here], dst_ref=into.at[h, e, here],
            send_sem=send.at[cell], recv_sem=recv.at[cell],
            device_id={"dom": target}, device_id_type=MESH)

    def rising(h, e, r):
        return hop(h, e, r, su, ru, u_send, u_recv, up)

    def falling(h, e, r):
        return hop(h, e, r, sd, rd, d_send, d_recv, down)

    def ends(t):
        return ((me, n - 1 - (t - me), rising, su, ru),
                (n - 1 - me, t - (n - 1 - me), falling, sd, rd))

    def own_flux(h):
        own = vx[blk, h]
        flux[h] = dot(own, st_hi[:rows, :]) + dot(own, st_lo[:rows, :])

    def couple(h):
        for side in range(2):
            onward[side, h].wait_recv()
        outer = jnp.concatenate(
            [jnp.concatenate([ht[side, h, c] for side in range(2)], axis=1) for c in range(2)], axis=0)
        total = flux[h] + dot(outer, st_hi[rows:, :]) + dot(outer, st_lo[rows:, :])
        return total.astype(BF16).T

    def multiply(h, b, u, columns):
        part[h, pl.ds(pl.multiple_of((2 * b + u) * half, half), half), :] = dot(vx[b, u], columns)

    order = [(t, h) for h in range(2) for t in range(n - 1)]

    def emit(i):
        t, h = order[i]
        for way, (first, e, make, out, into) in enumerate(ends(t)):
            @pl.when(first == 0)
            def _(way=way, e=e, make=make, out=out):
                if i >= 2:
                    t_done, h_done = order[i - 2]
                    e_done = ends(t_done)[way][1]
                    for r in range(pieces):
                        make(h_done, e_done, r).wait_send()
                for r in range(pieces):
                    out[h, e, r * piece:(r + 1) * piece] = term(h, e, r).astype(out.dtype)
                    make(h, e, r).start()

    own_flux(0)
    pass_halo(0)
    own_flux(1)
    pass_tiles(0)
    columns = couple(0)
    for u in range(2):
        multiply(0, blk, u, columns)
    for o in range(1, nblk):
        tiles_on[o, 0].wait_recv()
        multiply(0, source(o), x_half(source(o), 0), columns)
    emit(0)
    pass_halo(1)
    later = couple(1)
    pass_tiles(1)
    for u in range(2):
        multiply(1, blk, u, later)
    for o in range(1, nblk):
        multiply(1, source(o), x_half(source(o), 0), later)
    for o in range(1, nblk):
        tiles_on[o, 1].wait_recv()
        multiply(0, source(o), x_half(source(o), 1), columns)
    emit(1)
    for o in range(1, nblk):
        multiply(1, source(o), x_half(source(o), 1), later)
    for i in range(2, len(order)):
        emit(i)

    for h in range(2):
        for t in range(1, n - 1):
            for r in range(pieces):
                for first, e, make, out, into in ends(t):
                    @pl.when((first > 0) & (first <= t))
                    def _(r=r, e=e, make=make, out=out, into=into):
                        here = slice(r * piece, (r + 1) * piece)
                        make(h, e, r).wait_recv()
                        out[h, e, here] = (term(h, e, r) + into[h, e, here].astype(F32)).astype(out.dtype)
                        make(h, e, r).start()

        for r in range(pieces):
            here = slice(r * piece, (r + 1) * piece)
            there = slice(h * half, (h + 1) * half)

            @pl.when(me == 0)
            def _():
                falling(h, me, r).wait_recv()
                out_ref[here, there] = term(h, me, r) + rd[h, me, here].astype(F32)

            @pl.when(me == n - 1)
            def _():
                rising(h, me, r).wait_recv()
                out_ref[here, there] = term(h, me, r) + ru[h, me, here].astype(F32)

            @pl.when((me > 0) & (me < n - 1))
            def _():
                rising(h, me, r).wait_recv()
                falling(h, me, r).wait_recv()
                out_ref[here, there] = (
                    term(h, me, r) + ru[h, me, here].astype(F32) + rd[h, me, here].astype(F32))

    for i, (t, h) in enumerate(order):
        for first, e, make, out, into in ends(t):
            early = i < len(order) - 2

            @pl.when((first <= t) & (first > 0) if early else first <= t)
            def _(e=e, make=make):
                for r in range(pieces):
                    make(h, e, r).wait_send()

    for copy in [*halo.values(), *onward.values(), *tiles.values(), *tiles_on.values()]:
        copy.wait_send()


def paired(n, pieces, v_ref, force_ref, bond_ref, nbr_ref, low_ref, high_ref, out_ref,
           vbuf, vt, vx, perm, hs, ht, lp, fv, wq, bv, nv, lv, st_hi, st_lo, flux, turned, part,
           su, ru, se, re, in_sem, w_send, w_recv, wf_send, wf_recv, v_send, v_recv, vf_send, vf_recv,
           x_send, x_recv, xf_send, xf_recv, h_send, h_recv, hf_send, hf_recv,
           r_send, r_recv, e_send, e_recv):
    me = lax.axis_index("dom")
    blk = lax.axis_index("blk")
    core = lax.axis_index("dir")
    rows, cols = v_ref.shape
    atoms = rows // 3
    half = cols // 2
    share = half // 2
    bnd = low_ref.shape[1]
    steps = nbr_ref.shape[0]
    tile = out_ref.shape[0]
    piece = tile // pieces
    upper = me // 2
    mate = me + 1 - 2 * lax.rem(me, 2)
    other = n - 1 - me
    inner = (me > 0) & (me < n - 1)
    edge = (me == 0) | (me == n - 1)
    my_share = pl.ds(pl.multiple_of(core * share, share), share)
    lane_half = pl.ds(pl.multiple_of(core * (atoms // 2), atoms // 2), atoms // 2)

    def turn(b, p):
        return lax.rem(b + p, 2)

    def remote(src, dst, send, recv, target):
        return pltpu.make_async_remote_copy(
            src_ref=src, dst_ref=dst, send_sem=send, recv_sem=recv, device_id=target, device_id_type=MESH)

    barrier = pltpu.get_barrier_semaphore()

    def greet(*peers):
        for peer in peers:
            pl.semaphore_signal(barrier, inc=1, device_id=peer, device_id_type=MESH)

    fetch = pltpu.make_async_copy(v_ref, vbuf, in_sem.at[0])
    fetch.start()

    @pl.when(edge)
    def _():
        greet({"dom": mate})

    @pl.when(inner)
    def _():
        greet({"dom": mate}, {"dom": mate, "blk": 1 - blk}, {"dom": other}, {"dir": 1 - core}, {"blk": 1 - blk})

    row_of = lax.broadcasted_iota(jnp.int32, (rows, atoms), 0)
    atom_of = lax.broadcasted_iota(jnp.int32, (rows, atoms), 1)
    for a in range(3):
        perm[:, a * atoms:(a + 1) * atoms] = one_hot(row_of == 3 * atom_of + a)

    def sort_rows(c):
        picked = [vt[pl.ds(pl.multiple_of(h * half + c * share, share), share), :] for h in range(2)]
        sorted_rows = dot(jnp.concatenate(picked, axis=0), perm[...]).astype(BF16)
        for h in range(2):
            vx[0, blk, h, pl.ds(pl.multiple_of(c * share, share), share), :] = sorted_rows[h * share:(h + 1) * share]
        return sorted_rows

    weights = [
        remote(force_ref.at[:, :, lane_half], fv.at[1, :, :, lane_half], w_send.at[0], w_recv.at[0], {"dom": mate}),
        remote(bond_ref.at[0], bv.at[1], w_send.at[1], w_recv.at[1], {"dom": mate}),
        remote(nbr_ref, nv.at[1], w_send.at[2], w_recv.at[2], {"dom": mate}),
        remote(high_ref, lv.at[1, 0], w_send.at[3], w_recv.at[3], {"dom": mate}),
        remote(low_ref, lv.at[1, 1], w_send.at[4], w_recv.at[4], {"dom": mate}),
    ]
    panel = [
        remote(vx.at[0, blk, turn(blk, p), my_share], vx.at[1, blk, turn(blk, p), my_share],
               v_send.at[p], v_recv.at[p], {"dom": mate})
        for p in range(2)
    ]
    panel.append(
        remote(vx.at[0, blk, turn(blk, 1), my_share], vx.at[1, blk, turn(blk, 1), my_share],
               v_send.at[2], v_recv.at[2], {"dom": mate, "blk": 1 - blk}))

    def ending(i, r):
        here = pl.ds(r * piece, piece)
        cell = i * pieces + r
        return remote(se.at[i, here], re.at[i, here], e_send.at[cell], e_recv.at[cell], {"dom": mate})

    def columns_of(i):
        return pl.ds(pl.multiple_of(turn(blk, i) * half, half), half)

    @pl.when(edge)
    def _():
        pl.semaphore_wait(barrier, 2)
        for copy in weights:
            copy.start()
        fetch.wait()
        vt[...] = vbuf[...].T
        sort_rows(core)
        panel[0].start()
        panel[0].wait_send()
        panel[1].start()
        panel[1].wait_send()
        panel[2].start()
        for i in range(2):
            for r in range(pieces):
                ending(i, r).wait_recv()
                here = slice(r * piece, (r + 1) * piece)
                out_ref[here, columns_of(i)] = re[i, here].astype(F32)
        for copy in [*weights, panel[2]]:
            copy.wait_send()

    @pl.when(inner)
    def _():
        fetches = [
            pltpu.make_async_copy(high_ref, lv.at[0, 0], in_sem.at[1]),
            pltpu.make_async_copy(low_ref, lv.at[0, 1], in_sem.at[2]),
            pltpu.make_async_copy(nbr_ref, nv.at[0], in_sem.at[3]),
            pltpu.make_async_copy(bond_ref.at[0], bv.at[0], in_sem.at[4]),
            pltpu.make_async_copy(force_ref, fv.at[0], in_sem.at[5]),
        ]
        for copy in fetches:
            copy.start()
        fetches[0].wait()
        fetches[1].wait()
        atom_row = lax.broadcasted_iota(jnp.int32, (atoms, bnd), 0)

        def pick(d, which):
            return one_hot(atom_row == lv[d, which])

        def picked(source, chooser):
            return [dot(source[:, b * atoms:(b + 1) * atoms], chooser).astype(BF16) for b in range(3)]

        outward = pick(0, upper)
        fetch.wait()
        vt[...] = vbuf[...].T
        mine = sort_rows(core)
        for b, found in enumerate(picked(mine, outward)):
            for h in range(2):
                hs[0, turn(h, blk), :, b * bnd:(b + 1) * bnd] = found[h * share:(h + 1) * share]

        halo = {
            (kind, i): remote(hs.at[kind, i], ht.at[kind, i, core], h_send.at[2 * kind + i],
                              h_recv.at[2 * kind + i], {"dom": other})
            for kind in range(2) for i in range(2)
        }
        onward = {
            (kind, i): remote(ht.at[kind, i, core], ht.at[kind, i, core], hf_send.at[2 * kind + i],
                              hf_recv.at[2 * kind + i], {"dir": 1 - core})
            for kind in range(2) for i in range(2)
        }

        def across(d, p):
            at = vx.at[d, blk, turn(blk, p), my_share]
            return remote(at, at, x_send.at[2 * d + p], x_recv.at[2 * d + p], {"blk": 1 - blk})

        def across_on(d, p):
            at = vx.at[d, 1 - blk, turn(1 - blk, p), my_share]
            return remote(at, at, xf_send.at[2 * d + p], xf_recv.at[2 * d + p], {"dir": 1 - core})

        panel_on = [
            remote(vx.at[1, blk, turn(blk, p), my_share], vx.at[1, blk, turn(blk, p), my_share],
                   vf_send.at[p], vf_recv.at[p], {"dir": 1 - core})
            for p in range(2)
        ]
        force_on = remote(fv.at[1, :, :, lane_half], fv.at[1, :, :, lane_half],
                          wf_send.at[0], wf_recv.at[0], {"dir": 1 - core})

        pl.semaphore_wait(barrier, 4)
        halo[0, 0].start()
        across(0, 0).start()
        sort_rows(1 - core)

        def weigh(d):
            products = [fv[d, q] * bv[d] for q in range(9)]
            names = nv[d]
            k_of = lax.broadcasted_iota(jnp.int32, names.shape, 0)
            totals = list(products)
            for shift in range(1, steps):
                same = (names == pltpu.roll(names, shift, 0)) & (k_of >= shift)
                for q in range(9):
                    totals[q] = totals[q] + jnp.where(same, pltpu.roll(products[q], shift, 0), 0.0)
            for q in range(9):
                wq[q] = totals[q]

        sub, lanes, group = 8, 128, 32

        def build(d, first, count, base, stride):
            def body(t, carry):
                j0 = pl.multiple_of(t * group, group)
                for i0 in range(0, atoms, lanes):
                    here = slice(i0, i0 + lanes)
                    strips = range(group // sub)
                    js = [lax.broadcasted_iota(jnp.int32, (sub, lanes), 0) + (j0 + first + x * sub) for x in strips]
                    found = [jnp.full((sub, lanes), -1, jnp.int32) for _ in strips]
                    for k in range(steps):
                        name = jnp.broadcast_to(nv[d, k:k + 1, here], (sub, lanes))
                        for x in strips:
                            found[x] = jnp.where(js[x] == name, k, found[x])
                    spot = [f & (sub - 1) for f in found]
                    for a in range(3):
                        for b in range(3):
                            values = []
                            for x in strips:
                                value = jnp.zeros((sub, lanes), F32)
                                for k0 in range(0, steps, sub):
                                    taken = jnp.take_along_axis(
                                        wq[3 * a + b, k0:k0 + sub, here], spot[x], axis=0,
                                        mode="promise_in_bounds")
                                    value = jnp.where(found[x] >= k0, taken, value)
                                values.append(value)
                            value = jnp.concatenate(values, axis=0)
                            high = value.astype(BF16)
                            at = (d, pl.ds(pl.multiple_of(base + b * stride + j0, group), group),
                                  slice(a * atoms + i0, a * atoms + i0 + lanes))
                            st_hi[at] = high
                            st_lo[at] = (value - high.astype(F32)).astype(BF16)
                return carry

            lax.fori_loop(0, count // group, body, 0)

        def build_own(d):
            build(d, 0, atoms, 0, atoms)

        def build_outer(d):
            for place, side in ((0, upper), (1, 1 - upper)):
                build(d, atoms + side * bnd, bnd, rows + place * 3 * bnd, bnd)

        def own_flux(d, i):
            own = vx[d, blk, turn(blk, i)]
            flux[d, i] = dot(own, st_hi[d, :rows, :]) + dot(own, st_lo[d, :rows, :])

        def local(kind, d, i, which):
            for b, found in enumerate(picked(vx[d, blk, turn(blk, i)], pick(d, which))):
                lp[kind, i, :, b * bnd:(b + 1) * bnd] = found

        def couple(d, i):
            onward[d, i].wait_recv()
            came = jnp.concatenate([ht[d, i, c] for c in range(2)], axis=0)
            here = lp[d, i]
            outer = jnp.concatenate([here, came] if d == 0 else [came, here], axis=1)
            total = flux[d, i] + dot(outer, st_hi[d, rows:, :]) + dot(outer, st_lo[d, rows:, :])
            turned[i, d * rows:(d + 1) * rows, :] = total.astype(BF16).T

        def pass_halo(kind, i):
            halo[kind, i].wait_recv()
            onward[kind, i].start()

        def pass_panel(p):
            panel[p].wait_recv()
            panel_on[p].start()
            if p == 0:
                across(1, 0).start()
            source = vx[1, blk, turn(blk, p), my_share, :]
            for b, found in enumerate(picked(source, pick(1, 1 - upper))):
                hs[1, p, :, b * bnd:(b + 1) * bnd] = found
            halo[1, p].start()

        def pass_across(p):
            across(0, p).wait_recv()
            across_on(0, p).start()
            if p == 0:
                across(1, 0).wait_recv()
            else:
                panel[2].wait_recv()
            across_on(1, p).start()
            for d in range(2):
                across_on(d, p).wait_recv()

        def product(b, p, i, here):
            return (dot(vx[0, b, turn(b, p), here, :], turned[i, :rows, :])
                    + dot(vx[1, b, turn(b, p), here, :], turned[i, rows:, :]))

        def partial(p, i, r):
            here = pl.ds(r * piece, piece)
            cell = (2 * p + i) * pieces + r
            return remote(su.at[p, i, here], ru.at[p, i, here], r_send.at[cell], r_recv.at[cell], {"dom": other})

        away = 1 - upper

        def send(p, i):
            for r in range(pieces):
                here = slice(r * piece, (r + 1) * piece)
                su[p, i, here] = product(away, p, i, here).astype(BF16)
                partial(p, i, r).start()

        def keep(p, i):
            part[p, i] = product(upper, p, i, slice(0, tile))

        for copy in fetches[2:]:
            copy.wait()
        weigh(0)
        build_own(0)
        halo[0, 1].start()
        build_outer(0)
        pass_halo(0, 0)
        for i in range(2):
            own_flux(0, i)
            local(1, 0, i, 1 - upper)
        weights[0].wait_recv()
        force_on.start()
        for copy in weights[1:]:
            copy.wait_recv()
        pass_halo(0, 1)
        force_on.wait_recv()
        weigh(1)
        build_own(1)
        pass_panel(0)
        build_outer(1)
        panel_on[0].wait_recv()
        local(0, 1, 0, upper)
        own_flux(1, 0)
        couple(0, 0)
        pass_halo(1, 0)
        couple(1, 0)

        @pl.when(away == blk)
        def _():
            send(0, 0)

        pass_panel(1)
        pass_across(0)

        @pl.when(away != blk)
        def _():
            send(0, 0)

        across(1, 0).wait_send()
        across(0, 1).start()
        panel_on[1].wait_recv()
        local(0, 1, 1, upper)
        own_flux(1, 1)
        couple(0, 1)
        pass_halo(1, 1)
        couple(1, 1)
        send(0, 1)

        @pl.when(away == blk)
        def _():
            send(1, 0)
            send(1, 1)

        for i in range(2):
            keep(0, i)
        pass_across(1)

        @pl.when(away != blk)
        def _():
            send(1, 0)
            send(1, 1)

        for i in range(2):
            keep(1, i)

        for i in range(2):
            for r in range(pieces):
                here = slice(r * piece, (r + 1) * piece)
                partial(0, i, r).wait_recv()
                se[i, here] = (part[0, i, here] + ru[0, i, here].astype(F32)).astype(BF16)
                ending(i, r).start()
        for i in range(2):
            for r in range(pieces):
                here = slice(r * piece, (r + 1) * piece)
                partial(1, i, r).wait_recv()
                out_ref[here, columns_of(i)] = part[1, i, here] + ru[1, i, here].astype(F32)

        for copy in [*halo.values(), *onward.values(), across(0, 0), across(0, 1), *panel_on, force_on]:
            copy.wait_send()
        for d in range(2):
            for p in range(2):
                across_on(d, p).wait_send()
        for i in range(2):
            for r in range(pieces):
                ending(i, r).wait_send()
                for p in range(2):
                    partial(p, i, r).wait_send()


def paired_scratch(rows, cols, steps, bnd, tile, pieces):
    dma = pltpu.SemaphoreType.DMA
    atoms, half = rows // 3, cols // 2
    share = half // 2
    source = rows + 6 * bnd
    return [
        pltpu.VMEM((rows, cols), BF16),
        pltpu.VMEM((cols, rows), BF16),
        pltpu.VMEM((2, 2, 2, half, rows), BF16),
        pltpu.VMEM((rows, rows), BF16),
        pltpu.VMEM((2, 2, share, 3 * bnd), BF16),
        pltpu.VMEM((2, 2, 2, share, 3 * bnd), BF16),
        pltpu.VMEM((2, 2, half, 3 * bnd), BF16),
        pltpu.VMEM((2, 9, steps, atoms), F32),
        pltpu.VMEM((9, steps, atoms), F32),
        pltpu.VMEM((2, steps, atoms), F32),
        pltpu.VMEM((2, steps, atoms), jnp.int32),
        pltpu.VMEM((2, 2, 1, bnd), jnp.int32),
        pltpu.VMEM((2, source, rows), BF16),
        pltpu.VMEM((2, source, rows), BF16),
        pltpu.VMEM((2, 2, half, rows), F32),
        pltpu.VMEM((2, 2 * rows, half), BF16),
        pltpu.VMEM((2, 2, tile, half), F32),
        pltpu.VMEM((2, 2, tile, half), BF16),
        pltpu.VMEM((2, 2, tile, half), BF16),
        pltpu.VMEM((2, tile, half), BF16),
        pltpu.VMEM((2, tile, half), BF16),
        dma((6,)), dma((5,)), dma((5,)), dma((1,)), dma((1,)), dma((3,)), dma((3,)), dma((2,)), dma((2,)),
        dma((4,)), dma((4,)), dma((4,)), dma((4,)), dma((4,)), dma((4,)), dma((4,)), dma((4,)),
        dma((4 * pieces,)), dma((4 * pieces,)), dma((2 * pieces,)), dma((2 * pieces,)),
    ]


def per_device(n, nblk, panel_vectors, force_blocks, bond_vectors, neighbours, boundary_low, boundary_high):
    rows, cols = panel_vectors.shape
    atoms = rows // 3
    half = cols // 2
    bnd = boundary_low.shape[0]
    steps = neighbours.shape[0]
    tile = nblk * cols // n
    wire = BF16 if n <= 4 else F32
    vmem = pl.BlockSpec(memory_space=pltpu.VMEM)
    hbm = pl.BlockSpec(memory_space=pltpu.HBM)
    pieces = 2
    line = pltpu.VMEM((2, n, tile, half), wire)
    hops = pltpu.SemaphoreType.DMA((2 * n * pieces,))
    dma = pltpu.SemaphoreType.DMA
    shares = dma((2 * (nblk - 1),))
    if n == 4 and nblk == 2:
        body = functools.partial(paired, n, pieces)
        scratch = paired_scratch(rows, cols, steps, bnd, tile, pieces)
    else:
        body = functools.partial(kernel, n, nblk, pieces)
        scratch = [
            pltpu.VMEM((rows, cols), BF16),
            pltpu.VMEM((cols, rows), BF16),
            pltpu.VMEM((nblk, 2, half, rows), BF16),
            pltpu.VMEM((rows, rows), BF16),
            pltpu.VMEM((2, 2, half // 2, 3 * bnd), BF16),
            pltpu.VMEM((2, 2, 2, half // 2, 3 * bnd), BF16),
            pltpu.VMEM((9, steps, atoms), F32),
            pltpu.VMEM((9, steps, atoms), F32),
            pltpu.VMEM((steps, atoms), F32),
            pltpu.VMEM((steps, atoms), jnp.int32),
            pltpu.VMEM((2, 1, bnd), jnp.int32),
            pltpu.VMEM((rows + 6 * bnd, rows), BF16),
            pltpu.VMEM((rows + 6 * bnd, rows), BF16),
            pltpu.VMEM((2, half, rows), F32),
            pltpu.VMEM((2, nblk * cols, half), F32),
            line, line, line, line,
            dma((6,)), dma((4,)), dma((4,)), dma((4,)), dma((4,)),
            shares, shares, shares, shares,
            hops, hops, hops, hops,
        ]
    result = pl.pallas_call(
        body,
        out_shape=pltpu.VMEM((tile, cols), F32),
        in_specs=[hbm] * 6,
        out_specs=vmem,
        scratch_shapes=scratch,
        compiler_params=pltpu.CompilerParams(
            collective_id=0, has_side_effects=True, vmem_limit_bytes=48 * 1024 * 1024
        ),
    )(*[pltpu.with_memory_space_constraint(x, pltpu.HBM) for x in (
        panel_vectors, jnp.transpose(force_blocks, (1, 0, 2)), bond_vectors, neighbours,
        boundary_low.reshape(1, bnd), boundary_high.reshape(1, bnd))])
    scale = (3.0 * atoms * n) ** (-0.5)
    return (result * scale)[None, :, :]


def solution(mesh):
    in_specs = (
        P("dom", ("panel", "blk")),
        P(None, None, "dom"),
        P("dir", None, "dom"),
        P(None, "dom"),
        P("dom"),
        P("dom"),
    )
    out_specs = P("dir", ("panel", "dom"), "blk")
    return jax.shard_map(
        functools.partial(per_device, mesh.shape["dom"], mesh.shape["blk"]),
        mesh=mesh, in_specs=in_specs, out_specs=out_specs, check_vma=False
    )
```

```python
import functools

import jax
import jax.numpy as jnp
from jax import lax
from jax.experimental import pallas as pl
from jax.experimental.pallas import tpu as pltpu
from jax.sharding import PartitionSpec as P

MESH = pl.DeviceIdType.MESH
BF16 = jnp.bfloat16
F32 = jnp.float32


def one_hot(hits):
    return jnp.where(hits, 1.0, 0.0).astype(BF16)


def dot(a, b):
    return jnp.dot(a, b, preferred_element_type=F32)


def kernel(n, nblk, pieces, v_ref, force_ref, bond_ref, nbr_ref, low_ref, high_ref, out_ref,
           vbuf, vt, vx, perm, hs, ht, fv, wq, bv, nv, lv, st_hi, st_lo, flux, part, su, ru, sd, rd,
           in_sem, h_send, h_recv, hf_send, hf_recv, x_send, x_recv, xf_send, xf_recv,
           u_send, u_recv, d_send, d_recv):
    me = lax.axis_index("dom")
    blk = lax.axis_index("blk")
    core = lax.axis_index("dir")
    rows, cols = v_ref.shape
    atoms = rows // 3
    half = cols // 2
    share = half // 2
    bnd = low_ref.shape[1]
    steps = nbr_ref.shape[0]
    tile = out_ref.shape[0]
    piece = tile // pieces
    up, down = lax.rem(me + 1, n), lax.rem(me + n - 1, n)

    fetches = [
        pltpu.make_async_copy(high_ref, lv.at[0], in_sem.at[0]),
        pltpu.make_async_copy(low_ref, lv.at[1], in_sem.at[1]),
        pltpu.make_async_copy(v_ref, vbuf, in_sem.at[2]),
        pltpu.make_async_copy(nbr_ref, nv, in_sem.at[3]),
        pltpu.make_async_copy(bond_ref.at[0], bv, in_sem.at[4]),
        pltpu.make_async_copy(force_ref, fv, in_sem.at[5]),
    ]
    barrier = pltpu.get_barrier_semaphore()
    peers = [{"dom": up}, {"dom": down}, {"dir": 1 - core}]
    peers += [{"blk": lax.rem(blk + o, nblk)} for o in range(1, nblk)]
    for peer in peers:
        pl.semaphore_signal(barrier, inc=1, device_id=peer, device_id_type=MESH)
    for copy in fetches:
        copy.start()

    row_of = lax.broadcasted_iota(jnp.int32, (rows, atoms), 0)
    atom_of = lax.broadcasted_iota(jnp.int32, (rows, atoms), 1)
    for a in range(3):
        perm[:, a * atoms:(a + 1) * atoms] = one_hot(row_of == 3 * atom_of + a)
    fetches[0].wait()
    fetches[1].wait()
    atom_row = lax.broadcasted_iota(jnp.int32, (atoms, bnd), 0)
    pick = jnp.concatenate([one_hot(atom_row == lv[side]) for side in range(2)], axis=1)

    fetches[2].wait()
    vt[...] = vbuf[...].T

    def own_rows(c):
        return [pl.ds(pl.multiple_of(h * half + c * share, share), share) for h in range(2)]

    def sort_rows(c):
        sorted_rows = dot(jnp.concatenate([vt[r, :] for r in own_rows(c)], axis=0), perm[...]).astype(BF16)
        for h in range(2):
            vx[blk, h, pl.ds(pl.multiple_of(c * share, share), share), :] = sorted_rows[h * share:(h + 1) * share]
        return sorted_rows

    mine = sort_rows(core)
    for b in range(3):
        rows_out = dot(mine[:, b * atoms:(b + 1) * atoms], pick).astype(BF16)
        for side in range(2):
            for h in range(2):
                hs[side, h, :, b * bnd:(b + 1) * bnd] = rows_out[
                    h * share:(h + 1) * share, side * bnd:(side + 1) * bnd]
    pl.semaphore_wait(barrier, len(peers))

    halo = {
        (side, h): pltpu.make_async_remote_copy(
            src_ref=hs.at[side, h], dst_ref=ht.at[side, h, core],
            send_sem=h_send.at[2 * side + h], recv_sem=h_recv.at[2 * side + h],
            device_id={"dom": up if side == 0 else down}, device_id_type=MESH)
        for h in range(2) for side in range(2)
    }
    for side in range(2):
        halo[side, 0].start()

    my_share = pl.ds(pl.multiple_of(core * share, share), share)

    def x_half(b, p):
        return lax.rem(b + p, 2)

    tiles = {
        (o, p): pltpu.make_async_remote_copy(
            src_ref=vx.at[blk, x_half(blk, p), my_share], dst_ref=vx.at[blk, x_half(blk, p), my_share],
            send_sem=x_send.at[2 * (o - 1) + p], recv_sem=x_recv.at[2 * (o - 1) + p],
            device_id={"blk": lax.rem(blk + o, nblk)}, device_id_type=MESH)
        for o in range(1, nblk) for p in range(2)
    }
    for o in range(1, nblk):
        tiles[o, 0].start()
    sort_rows(1 - core)

    for i in range(3, 6):
        fetches[i].wait()
    for q in range(9):
        wq[q] = fv[q] * bv[...]
    names = nv[...]
    k_of = lax.broadcasted_iota(jnp.int32, names.shape, 0)
    totals = [wq[q] for q in range(9)]
    for s in range(1, steps):
        same = (names == pltpu.roll(names, s, 0)) & (k_of >= s)
        for q in range(9):
            totals[q] = totals[q] + jnp.where(same, pltpu.roll(wq[q], s, 0), 0.0)
    for q in range(9):
        wq[q] = totals[q]

    sub, lanes, group = 8, 128, 32

    def build(first, count, base, stride):
        def body(t, carry):
            j0 = pl.multiple_of(t * group, group)
            for i0 in range(0, atoms, lanes):
                here = slice(i0, i0 + lanes)
                strips = range(group // sub)
                js = [lax.broadcasted_iota(jnp.int32, (sub, lanes), 0) + (j0 + first + s * sub) for s in strips]
                found = [jnp.full((sub, lanes), -1, jnp.int32) for _ in strips]
                for k in range(steps):
                    name = jnp.broadcast_to(nv[k:k + 1, here], (sub, lanes))
                    for s in strips:
                        found[s] = jnp.where(js[s] == name, k, found[s])
                spot = [f & (sub - 1) for f in found]
                for a in range(3):
                    for b in range(3):
                        values = []
                        for s in strips:
                            value = jnp.zeros((sub, lanes), F32)
                            for k0 in range(0, steps, sub):
                                taken = jnp.take_along_axis(
                                    wq[3 * a + b, k0:k0 + sub, here], spot[s], axis=0, mode="promise_in_bounds")
                                value = jnp.where(found[s] >= k0, taken, value)
                            values.append(value)
                        value = jnp.concatenate(values, axis=0)
                        high = value.astype(BF16)
                        at = (pl.ds(pl.multiple_of(base + b * stride + j0, group), group),
                              slice(a * atoms + i0, a * atoms + i0 + lanes))
                        st_hi[at] = high
                        st_lo[at] = (value - high.astype(F32)).astype(BF16)
            return carry

        lax.fori_loop(0, count // group, body, 0)

    build(0, atoms, 0, atoms)
    for o in range(1, nblk):
        tiles[o, 1].start()
    build(atoms, bnd, rows, bnd)
    for side in range(2):
        halo[side, 1].start()
    build(atoms + bnd, bnd, rows + 3 * bnd, bnd)

    onward = {}
    tiles_on = {}

    def pass_halo(h):
        for side in range(2):
            halo[side, h].wait_recv()
            onward[side, h] = pltpu.make_async_remote_copy(
                src_ref=ht.at[side, h, core], dst_ref=ht.at[side, h, core],
                send_sem=hf_send.at[2 * side + h], recv_sem=hf_recv.at[2 * side + h],
                device_id={"dir": 1 - core}, device_id_type=MESH)
            onward[side, h].start()

    def source(o):
        return lax.rem(blk + nblk - o, nblk)

    def pass_tiles(p):
        for o in range(1, nblk):
            tiles[o, p].wait_recv()
            spot = (source(o), x_half(source(o), p), my_share)
            tiles_on[o, p] = pltpu.make_async_remote_copy(
                src_ref=vx.at[spot], dst_ref=vx.at[spot],
                send_sem=xf_send.at[2 * (o - 1) + p], recv_sem=xf_recv.at[2 * (o - 1) + p],
                device_id={"dir": 1 - core}, device_id_type=MESH)
            tiles_on[o, p].start()

    def term(h, e, r):
        return part[h, pl.ds(pl.multiple_of(e * tile + r * piece, piece), piece), :]

    def hop(h, e, r, out, into, send, recv, target):
        cell = (h * n + e) * pieces + r
        here = pl.ds(r * piece, piece)
        return pltpu.make_async_remote_copy(
            src_ref=out.at[h, e, here], dst_ref=into.at[h, e, here],
            send_sem=send.at[cell], recv_sem=recv.at[cell],
            device_id={"dom": target}, device_id_type=MESH)

    def rising(h, e, r):
        return hop(h, e, r, su, ru, u_send, u_recv, up)

    def falling(h, e, r):
        return hop(h, e, r, sd, rd, d_send, d_recv, down)

    def ends(t):
        return ((me, n - 1 - (t - me), rising, su, ru),
                (n - 1 - me, t - (n - 1 - me), falling, sd, rd))

    def own_flux(h):
        own = vx[blk, h]
        flux[h] = dot(own, st_hi[:rows, :]) + dot(own, st_lo[:rows, :])

    def couple(h):
        for side in range(2):
            onward[side, h].wait_recv()
        outer = jnp.concatenate(
            [jnp.concatenate([ht[side, h, c] for side in range(2)], axis=1) for c in range(2)], axis=0)
        total = flux[h] + dot(outer, st_hi[rows:, :]) + dot(outer, st_lo[rows:, :])
        return total.astype(BF16).T

    def multiply(h, b, u, columns):
        part[h, pl.ds(pl.multiple_of((2 * b + u) * half, half), half), :] = dot(vx[b, u], columns)

    order = [(t, h) for h in range(2) for t in range(n - 1)]

    def emit(i):
        t, h = order[i]
        for way, (first, e, make, out, into) in enumerate(ends(t)):
            @pl.when(first == 0)
            def _(way=way, e=e, make=make, out=out):
                if i >= 3:
                    t_done, h_done = order[i - 3]
                    e_done = ends(t_done)[way][1]
                    for r in range(pieces):
                        make(h_done, e_done, r).wait_send()
                for r in range(pieces):
                    out[h, e, r * piece:(r + 1) * piece] = term(h, e, r).astype(out.dtype)
                    make(h, e, r).start()

    own_flux(0)
    pass_halo(0)
    own_flux(1)
    pass_tiles(0)
    columns = couple(0)
    for u in range(2):
        multiply(0, blk, u, columns)
    for o in range(1, nblk):
        tiles_on[o, 0].wait_recv()
        multiply(0, source(o), x_half(source(o), 0), columns)
    emit(0)
    pass_halo(1)
    later = couple(1)
    pass_tiles(1)
    for u in range(2):
        multiply(1, blk, u, later)
    for o in range(1, nblk):
        multiply(1, source(o), x_half(source(o), 0), later)
    for o in range(1, nblk):
        tiles_on[o, 1].wait_recv()
        multiply(0, source(o), x_half(source(o), 1), columns)
    emit(1)
    for o in range(1, nblk):
        multiply(1, source(o), x_half(source(o), 1), later)
    for i in range(2, len(order)):
        emit(i)

    for h in range(2):
        for t in range(1, n - 1):
            for r in range(pieces):
                for first, e, make, out, into in ends(t):
                    @pl.when((first > 0) & (first <= t))
                    def _(r=r, e=e, make=make, out=out, into=into):
                        here = slice(r * piece, (r + 1) * piece)
                        make(h, e, r).wait_recv()
                        out[h, e, here] = (term(h, e, r) + into[h, e, here].astype(F32)).astype(out.dtype)
                        make(h, e, r).start()

        for r in range(pieces):
            here = slice(r * piece, (r + 1) * piece)
            there = slice(h * half, (h + 1) * half)

            @pl.when(me == 0)
            def _():
                falling(h, me, r).wait_recv()
                out_ref[here, there] = term(h, me, r) + rd[h, me, here].astype(F32)

            @pl.when(me == n - 1)
            def _():
                rising(h, me, r).wait_recv()
                out_ref[here, there] = term(h, me, r) + ru[h, me, here].astype(F32)

            @pl.when((me > 0) & (me < n - 1))
            def _():
                rising(h, me, r).wait_recv()
                falling(h, me, r).wait_recv()
                out_ref[here, there] = (
                    term(h, me, r) + ru[h, me, here].astype(F32) + rd[h, me, here].astype(F32))

    for i, (t, h) in enumerate(order):
        for first, e, make, out, into in ends(t):
            early = i < len(order) - 3

            @pl.when((first <= t) & (first > 0) if early else first <= t)
            def _(e=e, make=make):
                for r in range(pieces):
                    make(h, e, r).wait_send()

    for copy in [*halo.values(), *onward.values(), *tiles.values(), *tiles_on.values()]:
        copy.wait_send()


def per_device(n, nblk, panel_vectors, force_blocks, bond_vectors, neighbours, boundary_low, boundary_high):
    rows, cols = panel_vectors.shape
    atoms = rows // 3
    half = cols // 2
    bnd = boundary_low.shape[0]
    steps = neighbours.shape[0]
    tile = nblk * cols // n
    wire = BF16 if n <= 4 else F32
    vmem = pl.BlockSpec(memory_space=pltpu.VMEM)
    hbm = pl.BlockSpec(memory_space=pltpu.HBM)
    pieces = 4 if tile % 64 == 0 else 2
    line = pltpu.VMEM((2, n, tile, half), wire)
    hops = pltpu.SemaphoreType.DMA((2 * n * pieces,))
    dma = pltpu.SemaphoreType.DMA
    shares = dma((2 * (nblk - 1),))
    result = pl.pallas_call(
        functools.partial(kernel, n, nblk, pieces),
        out_shape=pltpu.VMEM((tile, cols), F32),
        in_specs=[hbm] * 6,
        out_specs=vmem,
        scratch_shapes=[
            pltpu.VMEM((rows, cols), BF16),
            pltpu.VMEM((cols, rows), BF16),
            pltpu.VMEM((nblk, 2, half, rows), BF16),
            pltpu.VMEM((rows, rows), BF16),
            pltpu.VMEM((2, 2, half // 2, 3 * bnd), BF16),
            pltpu.VMEM((2, 2, 2, half // 2, 3 * bnd), BF16),
            pltpu.VMEM((9, steps, atoms), F32),
            pltpu.VMEM((9, steps, atoms), F32),
            pltpu.VMEM((steps, atoms), F32),
            pltpu.VMEM((steps, atoms), jnp.int32),
            pltpu.VMEM((2, 1, bnd), jnp.int32),
            pltpu.VMEM((rows + 6 * bnd, rows), BF16),
            pltpu.VMEM((rows + 6 * bnd, rows), BF16),
            pltpu.VMEM((2, half, rows), F32),
            pltpu.VMEM((2, nblk * cols, half), F32),
            line, line, line, line,
            dma((6,)), dma((4,)), dma((4,)), dma((4,)), dma((4,)),
            shares, shares, shares, shares,
            hops, hops, hops, hops,
        ],
        compiler_params=pltpu.CompilerParams(
            collective_id=0, has_side_effects=True, vmem_limit_bytes=48 * 1024 * 1024
        ),
    )(*[pltpu.with_memory_space_constraint(x, pltpu.HBM) for x in (
        panel_vectors, jnp.transpose(force_blocks, (1, 0, 2)), bond_vectors, neighbours,
        boundary_low.reshape(1, bnd), boundary_high.reshape(1, bnd))])
    scale = (3.0 * atoms * n) ** (-0.5)
    return (result * scale)[None, :, :]


def solution(mesh):
    in_specs = (
        P("dom", ("panel", "blk")),
        P(None, None, "dom"),
        P("dir", None, "dom"),
        P(None, "dom"),
        P("dom"),
        P("dom"),
    )
    out_specs = P("dir", ("panel", "dom"), "blk")
    return jax.shard_map(
        functools.partial(per_device, mesh.shape["dom"], mesh.shape["blk"]),
        mesh=mesh, in_specs=in_specs, out_specs=out_specs, check_vma=False
    )
```

```python
import functools

import jax
import jax.numpy as jnp
from jax import lax
from jax.experimental import pallas as pl
from jax.experimental.pallas import tpu as pltpu
from jax.sharding import PartitionSpec as P

MESH = pl.DeviceIdType.MESH
BF16 = jnp.bfloat16
F32 = jnp.float32


def one_hot(hits):
    return jnp.where(hits, 1.0, 0.0).astype(BF16)


def dot(a, b):
    return jnp.dot(a, b, preferred_element_type=F32)


def kernel(n, nblk, pieces, v_ref, force_ref, bond_ref, nbr_ref, low_ref, high_ref, out_ref,
           vbuf, vt, vx, perm, hs, ht, fv, wq, bv, nv, lv, st_hi, st_lo, flux, part, su, ru, sd, rd,
           in_sem, h_send, h_recv, hf_send, hf_recv, x_send, x_recv, xf_send, xf_recv,
           u_send, u_recv, d_send, d_recv):
    me = lax.axis_index("dom")
    blk = lax.axis_index("blk")
    core = lax.axis_index("dir")
    rows, cols = v_ref.shape
    atoms = rows // 3
    half = cols // 2
    share = half // 2
    bnd = low_ref.shape[1]
    steps = nbr_ref.shape[0]
    tile = out_ref.shape[0]
    piece = tile // pieces
    up, down = lax.rem(me + 1, n), lax.rem(me + n - 1, n)

    def columns_of(c, h):
        return pl.ds(pl.multiple_of(h * half + c * share, share), share)

    fetches = [
        pltpu.make_async_copy(high_ref, lv.at[0], in_sem.at[0]),
        pltpu.make_async_copy(low_ref, lv.at[1], in_sem.at[1]),
        pltpu.make_async_copy(nbr_ref, nv, in_sem.at[2]),
        pltpu.make_async_copy(bond_ref.at[0], bv, in_sem.at[3]),
        pltpu.make_async_copy(force_ref, fv, in_sem.at[4]),
    ]
    by_columns = share % 128 == 0
    if by_columns:
        panel = [
            pltpu.make_async_copy(v_ref.at[:, columns_of(c, h)], vbuf.at[:, columns_of(c, h)], in_sem.at[5 + i])
            for i, (c, h) in enumerate(((core, 0), (core, 1), (1 - core, 0), (1 - core, 1)))
        ]
    else:
        panel = [pltpu.make_async_copy(v_ref, vbuf, in_sem.at[5])]
    barrier = pltpu.get_barrier_semaphore()
    peers = [{"dom": up}, {"dom": down}, {"dir": 1 - core}]
    peers += [{"blk": lax.rem(blk + o, nblk)} for o in range(1, nblk)]
    for peer in peers:
        pl.semaphore_signal(barrier, inc=1, device_id=peer, device_id_type=MESH)
    for copy in [*fetches[:2], *panel, *fetches[2:]]:
        copy.start()

    row_of = lax.broadcasted_iota(jnp.int32, (rows, atoms), 0)
    atom_of = lax.broadcasted_iota(jnp.int32, (rows, atoms), 1)
    for a in range(3):
        perm[:, a * atoms:(a + 1) * atoms] = one_hot(row_of == 3 * atom_of + a)
    fetches[0].wait()
    fetches[1].wait()
    atom_row = lax.broadcasted_iota(jnp.int32, (atoms, bnd), 0)
    pick = jnp.concatenate([one_hot(atom_row == lv[side]) for side in range(2)], axis=1)

    def sort_rows(c):
        if by_columns:
            turned = [vbuf[:, columns_of(c, h)].T for h in range(2)]
        else:
            turned = [vt[columns_of(c, h), :] for h in range(2)]
        turned = jnp.concatenate(turned, axis=0)
        sorted_rows = dot(turned, perm[...]).astype(BF16)
        for h in range(2):
            vx[blk, h, pl.ds(pl.multiple_of(c * share, share), share), :] = sorted_rows[h * share:(h + 1) * share]
        return sorted_rows

    for copy in panel[:2]:
        copy.wait()
    if not by_columns:
        vt[...] = vbuf[...].T
    mine = sort_rows(core)
    for b in range(3):
        rows_out = dot(mine[:, b * atoms:(b + 1) * atoms], pick).astype(BF16)
        for side in range(2):
            for h in range(2):
                hs[side, h, :, b * bnd:(b + 1) * bnd] = rows_out[
                    h * share:(h + 1) * share, side * bnd:(side + 1) * bnd]
    pl.semaphore_wait(barrier, len(peers))

    halo = {
        (side, h): pltpu.make_async_remote_copy(
            src_ref=hs.at[side, h], dst_ref=ht.at[side, h, core],
            send_sem=h_send.at[2 * side + h], recv_sem=h_recv.at[2 * side + h],
            device_id={"dom": up if side == 0 else down}, device_id_type=MESH)
        for h in range(2) for side in range(2)
    }
    for side in range(2):
        halo[side, 0].start()

    my_share = pl.ds(pl.multiple_of(core * share, share), share)

    def x_half(b, p):
        return lax.rem(b + p, 2)

    tiles = {
        (o, p): pltpu.make_async_remote_copy(
            src_ref=vx.at[blk, x_half(blk, p), my_share], dst_ref=vx.at[blk, x_half(blk, p), my_share],
            send_sem=x_send.at[2 * (o - 1) + p], recv_sem=x_recv.at[2 * (o - 1) + p],
            device_id={"blk": lax.rem(blk + o, nblk)}, device_id_type=MESH)
        for o in range(1, nblk) for p in range(2)
    }
    for o in range(1, nblk):
        tiles[o, 0].start()
    for copy in panel[2:]:
        copy.wait()
    sort_rows(1 - core)

    for copy in fetches[2:]:
        copy.wait()
    for q in range(9):
        wq[q] = fv[q] * bv[...]
    names = nv[...]
    k_of = lax.broadcasted_iota(jnp.int32, names.shape, 0)
    totals = [wq[q] for q in range(9)]
    for s in range(1, steps):
        same = (names == pltpu.roll(names, s, 0)) & (k_of >= s)
        for q in range(9):
            totals[q] = totals[q] + jnp.where(same, pltpu.roll(wq[q], s, 0), 0.0)
    for q in range(9):
        wq[q] = totals[q]

    sub, lanes, group = 8, 128, 32

    def build(first, count, base, stride):
        def body(t, carry):
            j0 = pl.multiple_of(t * group, group)
            for i0 in range(0, atoms, lanes):
                here = slice(i0, i0 + lanes)
                strips = range(group // sub)
                js = [lax.broadcasted_iota(jnp.int32, (sub, lanes), 0) + (j0 + first + s * sub) for s in strips]
                found = [jnp.full((sub, lanes), -1, jnp.int32) for _ in strips]
                for k in range(steps):
                    name = jnp.broadcast_to(nv[k:k + 1, here], (sub, lanes))
                    for s in strips:
                        found[s] = jnp.where(js[s] == name, k, found[s])
                spot = [f & (sub - 1) for f in found]
                for a in range(3):
                    for b in range(3):
                        values = []
                        for s in strips:
                            value = jnp.zeros((sub, lanes), F32)
                            for k0 in range(0, steps, sub):
                                taken = jnp.take_along_axis(
                                    wq[3 * a + b, k0:k0 + sub, here], spot[s], axis=0, mode="promise_in_bounds")
                                value = jnp.where(found[s] >= k0, taken, value)
                            values.append(value)
                        value = jnp.concatenate(values, axis=0)
                        high = value.astype(BF16)
                        at = (pl.ds(pl.multiple_of(base + b * stride + j0, group), group),
                              slice(a * atoms + i0, a * atoms + i0 + lanes))
                        st_hi[at] = high
                        st_lo[at] = (value - high.astype(F32)).astype(BF16)
            return carry

        lax.fori_loop(0, count // group, body, 0)

    build(0, atoms, 0, atoms)
    for o in range(1, nblk):
        tiles[o, 1].start()
    build(atoms, bnd, rows, bnd)
    build(atoms + bnd, bnd, rows + 3 * bnd, bnd)
    for side in range(2):
        halo[side, 1].start()

    onward = {}
    tiles_on = {}

    def pass_halo(h):
        for side in range(2):
            halo[side, h].wait_recv()
            onward[side, h] = pltpu.make_async_remote_copy(
                src_ref=ht.at[side, h, core], dst_ref=ht.at[side, h, core],
                send_sem=hf_send.at[2 * side + h], recv_sem=hf_recv.at[2 * side + h],
                device_id={"dir": 1 - core}, device_id_type=MESH)
            onward[side, h].start()

    def source(o):
        return lax.rem(blk + nblk - o, nblk)

    def pass_tiles(p):
        for o in range(1, nblk):
            tiles[o, p].wait_recv()
            spot = (source(o), x_half(source(o), p), my_share)
            tiles_on[o, p] = pltpu.make_async_remote_copy(
                src_ref=vx.at[spot], dst_ref=vx.at[spot],
                send_sem=xf_send.at[2 * (o - 1) + p], recv_sem=xf_recv.at[2 * (o - 1) + p],
                device_id={"dir": 1 - core}, device_id_type=MESH)
            tiles_on[o, p].start()

    def term(h, e, r):
        return part[h, pl.ds(pl.multiple_of(e * tile + r * piece, piece), piece), :]

    def hop(h, e, r, out, into, send, recv, target):
        cell = (h * n + e) * pieces + r
        here = pl.ds(r * piece, piece)
        return pltpu.make_async_remote_copy(
            src_ref=out.at[h, e, here], dst_ref=into.at[h, e, here],
            send_sem=send.at[cell], recv_sem=recv.at[cell],
            device_id={"dom": target}, device_id_type=MESH)

    def rising(h, e, r):
        return hop(h, e, r, su, ru, u_send, u_recv, up)

    def falling(h, e, r):
        return hop(h, e, r, sd, rd, d_send, d_recv, down)

    def ends(t):
        return ((me, n - 1 - (t - me), rising, su, ru),
                (n - 1 - me, t - (n - 1 - me), falling, sd, rd))

    def own_flux(h):
        own = vx[blk, h]
        flux[h] = dot(own, st_hi[:rows, :]) + dot(own, st_lo[:rows, :])

    def couple(h):
        for side in range(2):
            onward[side, h].wait_recv()
        outer = jnp.concatenate(
            [jnp.concatenate([ht[side, h, c] for side in range(2)], axis=1) for c in range(2)], axis=0)
        total = flux[h] + dot(outer, st_hi[rows:, :]) + dot(outer, st_lo[rows:, :])
        return total.astype(BF16).T

    def multiply(h, b, u, columns):
        part[h, pl.ds(pl.multiple_of((2 * b + u) * half, half), half), :] = dot(vx[b, u], columns)

    far, near = (blk == nblk - 1, blk == 0), (blk < nblk - 1, blk > 0)
    always = (True, True)
    if n == 4 and nblk == 2:
        first_part, second_part, third_part = [(0, far), (1, far), (2, near)], [(0, near)], [(2, far), (1, near)]
    else:
        first_part, second_part, third_part = [], [], [(t, always) for t in range(n - 1)]

    def emit(t, h, where):
        for (first, e, make, out, into), here in zip(ends(t), where):
            @pl.when((first == 0) & here)
            def _(e=e, make=make, out=out):
                if h == 1:
                    for r in range(pieces):
                        make(0, e, r).wait_send()
                for r in range(pieces):
                    out[h, e, r * piece:(r + 1) * piece] = term(h, e, r).astype(out.dtype)
                    make(h, e, r).start()

    own_flux(0)
    own_flux(1)
    pass_halo(0)
    columns = couple(0)
    for u in range(2):
        multiply(0, blk, u, columns)
    for t, where in first_part:
        emit(t, 0, where)
    pass_tiles(0)
    for o in range(1, nblk):
        tiles_on[o, 0].wait_recv()
        multiply(0, source(o), x_half(source(o), 0), columns)
    for t, where in second_part:
        emit(t, 0, where)
    pass_tiles(1)
    pass_halo(1)
    for o in range(1, nblk):
        tiles_on[o, 1].wait_recv()
        multiply(0, source(o), x_half(source(o), 1), columns)
    for t, where in third_part:
        emit(t, 0, where)
    later = couple(1)
    for u in range(2):
        multiply(1, blk, u, later)
    for o in range(1, nblk):
        for p in range(2):
            multiply(1, source(o), x_half(source(o), p), later)
    for t in range(n - 1):
        emit(t, 1, always)

    for h in range(2):
        for t in range(1, n - 1):
            for r in range(pieces):
                for first, e, make, out, into in ends(t):
                    @pl.when((first > 0) & (first <= t))
                    def _(r=r, e=e, make=make, out=out, into=into):
                        here = slice(r * piece, (r + 1) * piece)
                        make(h, e, r).wait_recv()
                        out[h, e, here] = (term(h, e, r) + into[h, e, here].astype(F32)).astype(out.dtype)
                        make(h, e, r).start()

        for r in range(pieces):
            here = slice(r * piece, (r + 1) * piece)
            there = slice(h * half, (h + 1) * half)

            @pl.when(me == 0)
            def _():
                falling(h, me, r).wait_recv()
                out_ref[here, there] = term(h, me, r) + rd[h, me, here].astype(F32)

            @pl.when(me == n - 1)
            def _():
                rising(h, me, r).wait_recv()
                out_ref[here, there] = term(h, me, r) + ru[h, me, here].astype(F32)

            @pl.when((me > 0) & (me < n - 1))
            def _():
                rising(h, me, r).wait_recv()
                falling(h, me, r).wait_recv()
                out_ref[here, there] = (
                    term(h, me, r) + ru[h, me, here].astype(F32) + rd[h, me, here].astype(F32))

    for h in range(2):
        for t in range(n - 1):
            for first, e, make, out, into in ends(t):
                @pl.when((first <= t) & (first > 0) if h == 0 else first <= t)
                def _(e=e, make=make):
                    for r in range(pieces):
                        make(h, e, r).wait_send()

    for copy in [*halo.values(), *onward.values(), *tiles.values(), *tiles_on.values()]:
        copy.wait_send()


def per_device(n, nblk, panel_vectors, force_blocks, bond_vectors, neighbours, boundary_low, boundary_high):
    rows, cols = panel_vectors.shape
    atoms = rows // 3
    half = cols // 2
    bnd = boundary_low.shape[0]
    steps = neighbours.shape[0]
    tile = nblk * cols // n
    wire = BF16 if n <= 4 else F32
    vmem = pl.BlockSpec(memory_space=pltpu.VMEM)
    hbm = pl.BlockSpec(memory_space=pltpu.HBM)
    pieces = 4 if tile % 64 == 0 else 2
    line = pltpu.VMEM((2, n, tile, half), wire)
    hops = pltpu.SemaphoreType.DMA((2 * n * pieces,))
    dma = pltpu.SemaphoreType.DMA
    shares = dma((2 * (nblk - 1),))
    result = pl.pallas_call(
        functools.partial(kernel, n, nblk, pieces),
        out_shape=pltpu.VMEM((tile, cols), F32),
        in_specs=[hbm] * 6,
        out_specs=vmem,
        scratch_shapes=[
            pltpu.VMEM((rows, cols), BF16),
            pltpu.VMEM((cols, rows), BF16),
            pltpu.VMEM((nblk, 2, half, rows), BF16),
            pltpu.VMEM((rows, rows), BF16),
            pltpu.VMEM((2, 2, half // 2, 3 * bnd), BF16),
            pltpu.VMEM((2, 2, 2, half // 2, 3 * bnd), BF16),
            pltpu.VMEM((9, steps, atoms), F32),
            pltpu.VMEM((9, steps, atoms), F32),
            pltpu.VMEM((steps, atoms), F32),
            pltpu.VMEM((steps, atoms), jnp.int32),
            pltpu.VMEM((2, 1, bnd), jnp.int32),
            pltpu.VMEM((rows + 6 * bnd, rows), BF16),
            pltpu.VMEM((rows + 6 * bnd, rows), BF16),
            pltpu.VMEM((2, half, rows), F32),
            pltpu.VMEM((2, nblk * cols, half), F32),
            line, line, line, line,
            dma((9,)), dma((4,)), dma((4,)), dma((4,)), dma((4,)),
            shares, shares, shares, shares,
            hops, hops, hops, hops,
        ],
        compiler_params=pltpu.CompilerParams(
            collective_id=0, has_side_effects=True, vmem_limit_bytes=48 * 1024 * 1024
        ),
    )(*[pltpu.with_memory_space_constraint(x, pltpu.HBM) for x in (
        panel_vectors, jnp.transpose(force_blocks, (1, 0, 2)), bond_vectors, neighbours,
        boundary_low.reshape(1, bnd), boundary_high.reshape(1, bnd))])
    scale = (3.0 * atoms * n) ** (-0.5)
    return (result * scale)[None, :, :]


def solution(mesh):
    in_specs = (
        P("dom", ("panel", "blk")),
        P(None, None, "dom"),
        P("dir", None, "dom"),
        P(None, "dom"),
        P("dom"),
        P("dom"),
    )
    out_specs = P("dir", ("panel", "dom"), "blk")
    return jax.shard_map(
        functools.partial(per_device, mesh.shape["dom"], mesh.shape["blk"]),
        mesh=mesh, in_specs=in_specs, out_specs=out_specs, check_vma=False
    )
```

```python
import functools

import jax
import jax.numpy as jnp
from jax import lax
from jax.experimental import pallas as pl
from jax.experimental.pallas import tpu as pltpu
from jax.sharding import PartitionSpec as P

MESH = pl.DeviceIdType.MESH
BF16 = jnp.bfloat16
F32 = jnp.float32


def one_hot(hits):
    return jnp.where(hits, 1.0, 0.0).astype(BF16)


def dot(a, b):
    return jnp.dot(a, b, preferred_element_type=F32)


def kernel(n, nblk, pieces, v_ref, force_ref, bond_ref, nbr_ref, low_ref, high_ref, out_ref,
           vbuf, vt, vx, perm, hs, ht, fv, wq, bv, nv, lv, st_hi, st_lo, flux, part, su, ru, sd, rd,
           in_sem, h_send, h_recv, hf_send, hf_recv, x_send, x_recv, xf_send, xf_recv,
           u_send, u_recv, d_send, d_recv):
    me = lax.axis_index("dom")
    blk = lax.axis_index("blk")
    core = lax.axis_index("dir")
    rows, cols = v_ref.shape
    atoms = rows // 3
    half = cols // 2
    share = half // 2
    bnd = low_ref.shape[1]
    steps = nbr_ref.shape[0]
    tile = out_ref.shape[0]
    piece = tile // pieces
    up, down = lax.rem(me + 1, n), lax.rem(me + n - 1, n)

    def columns_of(c, h):
        return pl.ds(pl.multiple_of(h * half + c * share, share), share)

    fetches = [
        pltpu.make_async_copy(high_ref, lv.at[0], in_sem.at[0]),
        pltpu.make_async_copy(low_ref, lv.at[1], in_sem.at[1]),
        pltpu.make_async_copy(nbr_ref, nv, in_sem.at[2]),
        pltpu.make_async_copy(bond_ref.at[0], bv, in_sem.at[3]),
        pltpu.make_async_copy(force_ref, fv, in_sem.at[4]),
    ]
    by_columns = share % 128 == 0
    if by_columns:
        panel = [
            pltpu.make_async_copy(v_ref.at[:, columns_of(c, h)], vbuf.at[:, columns_of(c, h)], in_sem.at[5 + i])
            for i, (c, h) in enumerate(((core, 0), (core, 1), (1 - core, 0), (1 - core, 1)))
        ]
    else:
        panel = [pltpu.make_async_copy(v_ref, vbuf, in_sem.at[5])]
    barrier = pltpu.get_barrier_semaphore()
    peers = [{"dom": up}, {"dom": down}, {"dir": 1 - core}]
    peers += [{"blk": lax.rem(blk + o, nblk)} for o in range(1, nblk)]
    for peer in peers:
        pl.semaphore_signal(barrier, inc=1, device_id=peer, device_id_type=MESH)
    for copy in [*fetches[:2], *panel, *fetches[2:]]:
        copy.start()

    row_of = lax.broadcasted_iota(jnp.int32, (rows, atoms), 0)
    atom_of = lax.broadcasted_iota(jnp.int32, (rows, atoms), 1)
    for a in range(3):
        perm[:, a * atoms:(a + 1) * atoms] = one_hot(row_of == 3 * atom_of + a)
    fetches[0].wait()
    fetches[1].wait()
    atom_row = lax.broadcasted_iota(jnp.int32, (atoms, bnd), 0)
    pick = jnp.concatenate([one_hot(atom_row == lv[side]) for side in range(2)], axis=1)

    def sort_rows(c):
        if by_columns:
            turned = [vbuf[:, columns_of(c, h)].T for h in range(2)]
        else:
            turned = [vt[columns_of(c, h), :] for h in range(2)]
        turned = jnp.concatenate(turned, axis=0)
        sorted_rows = dot(turned, perm[...]).astype(BF16)
        for h in range(2):
            vx[blk, h, pl.ds(pl.multiple_of(c * share, share), share), :] = sorted_rows[h * share:(h + 1) * share]
        return sorted_rows

    for copy in panel[:2]:
        copy.wait()
    if not by_columns:
        vt[...] = vbuf[...].T
    mine = sort_rows(core)
    for b in range(3):
        rows_out = dot(mine[:, b * atoms:(b + 1) * atoms], pick).astype(BF16)
        for side in range(2):
            for h in range(2):
                hs[side, h, :, b * bnd:(b + 1) * bnd] = rows_out[
                    h * share:(h + 1) * share, side * bnd:(side + 1) * bnd]
    pl.semaphore_wait(barrier, len(peers))

    halo = {
        (side, h): pltpu.make_async_remote_copy(
            src_ref=hs.at[side, h], dst_ref=ht.at[side, h, core],
            send_sem=h_send.at[2 * side + h], recv_sem=h_recv.at[2 * side + h],
            device_id={"dom": up if side == 0 else down}, device_id_type=MESH)
        for h in range(2) for side in range(2)
    }
    for side in range(2):
        halo[side, 0].start()

    my_share = pl.ds(pl.multiple_of(core * share, share), share)

    def x_half(b, p):
        return lax.rem(b + p, 2)

    tiles = {
        (o, p): pltpu.make_async_remote_copy(
            src_ref=vx.at[blk, x_half(blk, p), my_share], dst_ref=vx.at[blk, x_half(blk, p), my_share],
            send_sem=x_send.at[2 * (o - 1) + p], recv_sem=x_recv.at[2 * (o - 1) + p],
            device_id={"blk": lax.rem(blk + o, nblk)}, device_id_type=MESH)
        for o in range(1, nblk) for p in range(2)
    }
    for o in range(1, nblk):
        tiles[o, 0].start()
    for copy in panel[2:]:
        copy.wait()
    sort_rows(1 - core)

    for copy in fetches[2:]:
        copy.wait()
    for q in range(9):
        wq[q] = fv[q] * bv[...]
    names = nv[...]
    k_of = lax.broadcasted_iota(jnp.int32, names.shape, 0)
    totals = [wq[q] for q in range(9)]
    for s in range(1, steps):
        same = (names == pltpu.roll(names, s, 0)) & (k_of >= s)
        for q in range(9):
            totals[q] = totals[q] + jnp.where(same, pltpu.roll(wq[q], s, 0), 0.0)
    for q in range(9):
        wq[q] = totals[q]

    sub, lanes, group = 8, 128, 32

    def build(first, count, base, stride):
        def body(t, carry):
            j0 = pl.multiple_of(t * group, group)
            for i0 in range(0, atoms, lanes):
                here = slice(i0, i0 + lanes)
                strips = range(group // sub)
                js = [lax.broadcasted_iota(jnp.int32, (sub, lanes), 0) + (j0 + first + s * sub) for s in strips]
                found = [jnp.full((sub, lanes), -1, jnp.int32) for _ in strips]
                for k in range(steps):
                    name = jnp.broadcast_to(nv[k:k + 1, here], (sub, lanes))
                    for s in strips:
                        found[s] = jnp.where(js[s] == name, k, found[s])
                spot = [f & (sub - 1) for f in found]
                for a in range(3):
                    for b in range(3):
                        values = []
                        for s in strips:
                            value = jnp.zeros((sub, lanes), F32)
                            for k0 in range(0, steps, sub):
                                taken = jnp.take_along_axis(
                                    wq[3 * a + b, k0:k0 + sub, here], spot[s], axis=0, mode="promise_in_bounds")
                                value = jnp.where(found[s] >= k0, taken, value)
                            values.append(value)
                        value = jnp.concatenate(values, axis=0)
                        high = value.astype(BF16)
                        at = (pl.ds(pl.multiple_of(base + b * stride + j0, group), group),
                              slice(a * atoms + i0, a * atoms + i0 + lanes))
                        st_hi[at] = high
                        st_lo[at] = (value - high.astype(F32)).astype(BF16)
            return carry

        lax.fori_loop(0, count // group, body, 0)

    build(0, atoms, 0, atoms)
    for o in range(1, nblk):
        tiles[o, 1].start()
    build(atoms, bnd, rows, bnd)
    build(atoms + bnd, bnd, rows + 3 * bnd, bnd)
    for side in range(2):
        halo[side, 1].start()

    onward = {}
    tiles_on = {}

    def pass_halo(h):
        for side in range(2):
            halo[side, h].wait_recv()
            onward[side, h] = pltpu.make_async_remote_copy(
                src_ref=ht.at[side, h, core], dst_ref=ht.at[side, h, core],
                send_sem=hf_send.at[2 * side + h], recv_sem=hf_recv.at[2 * side + h],
                device_id={"dir": 1 - core}, device_id_type=MESH)
            onward[side, h].start()

    def source(o):
        return lax.rem(blk + nblk - o, nblk)

    def pass_tiles(p):
        for o in range(1, nblk):
            tiles[o, p].wait_recv()
            spot = (source(o), x_half(source(o), p), my_share)
            tiles_on[o, p] = pltpu.make_async_remote_copy(
                src_ref=vx.at[spot], dst_ref=vx.at[spot],
                send_sem=xf_send.at[2 * (o - 1) + p], recv_sem=xf_recv.at[2 * (o - 1) + p],
                device_id={"dir": 1 - core}, device_id_type=MESH)
            tiles_on[o, p].start()

    def term(h, e, r):
        return part[h, pl.ds(pl.multiple_of(e * tile + r * piece, piece), piece), :]

    def hop(h, e, r, out, into, send, recv, target):
        cell = (h * n + e) * pieces + r
        here = pl.ds(r * piece, piece)
        return pltpu.make_async_remote_copy(
            src_ref=out.at[h, e, here], dst_ref=into.at[h, e, here],
            send_sem=send.at[cell], recv_sem=recv.at[cell],
            device_id={"dom": target}, device_id_type=MESH)

    def rising(h, e, r):
        return hop(h, e, r, su, ru, u_send, u_recv, up)

    def falling(h, e, r):
        return hop(h, e, r, sd, rd, d_send, d_recv, down)

    def ends(t):
        return ((me, n - 1 - (t - me), rising, su, ru),
                (n - 1 - me, t - (n - 1 - me), falling, sd, rd))

    def own_flux(h):
        own = vx[blk, h]
        flux[h] = dot(own, st_hi[:rows, :]) + dot(own, st_lo[:rows, :])

    def couple(h):
        for side in range(2):
            onward[side, h].wait_recv()
        outer = jnp.concatenate(
            [jnp.concatenate([ht[side, h, c] for side in range(2)], axis=1) for c in range(2)], axis=0)
        total = flux[h] + dot(outer, st_hi[rows:, :]) + dot(outer, st_lo[rows:, :])
        return total.astype(BF16).T

    def multiply(h, b, u, columns):
        part[h, pl.ds(pl.multiple_of((2 * b + u) * half, half), half), :] = dot(vx[b, u], columns)

    far, near = (blk == nblk - 1, blk == 0), (blk < nblk - 1, blk > 0)
    always = (True, True)
    if n == 4 and nblk == 2:
        first_part, second_part, third_part = [(0, far), (1, far), (2, near)], [(0, near)], [(2, far), (1, near)]
    else:
        first_part, second_part, third_part = [], [], [(t, always) for t in range(n - 1)]

    def emit(t, h, where):
        for (first, e, make, out, into), here in zip(ends(t), where):
            @pl.when((first == 0) & here)
            def _(e=e, make=make, out=out):
                if h == 1:
                    for r in range(pieces):
                        make(0, e, r).wait_send()
                for r in range(pieces):
                    out[h, e, r * piece:(r + 1) * piece] = term(h, e, r).astype(out.dtype)
                    make(h, e, r).start()

    def forward(h):
        for t in range(1, n - 1):
            for r in range(pieces):
                for first, e, make, out, into in ends(t):
                    @pl.when((first > 0) & (first <= t))
                    def _(r=r, e=e, make=make, out=out, into=into):
                        here = slice(r * piece, (r + 1) * piece)
                        make(h, e, r).wait_recv()
                        out[h, e, here] = (term(h, e, r) + into[h, e, here].astype(F32)).astype(out.dtype)
                        make(h, e, r).start()

    own_flux(0)
    own_flux(1)
    pass_halo(0)
    columns = couple(0)
    for u in range(2):
        multiply(0, blk, u, columns)
    for t, where in first_part:
        emit(t, 0, where)
    pass_tiles(0)
    for o in range(1, nblk):
        tiles_on[o, 0].wait_recv()
        multiply(0, source(o), x_half(source(o), 0), columns)
    for t, where in second_part:
        emit(t, 0, where)
    pass_tiles(1)
    pass_halo(1)
    for o in range(1, nblk):
        tiles_on[o, 1].wait_recv()
        multiply(0, source(o), x_half(source(o), 1), columns)
    for t, where in third_part:
        emit(t, 0, where)
    later = couple(1)
    forward(0)
    for u in range(2):
        multiply(1, blk, u, later)
    for o in range(1, nblk):
        for p in range(2):
            multiply(1, source(o), x_half(source(o), p), later)
    for t in range(n - 1):
        emit(t, 1, always)
    forward(1)

    for h in range(2):
        for r in range(pieces):
            here = slice(r * piece, (r + 1) * piece)
            there = slice(h * half, (h + 1) * half)

            @pl.when(me == 0)
            def _():
                falling(h, me, r).wait_recv()
                out_ref[here, there] = term(h, me, r) + rd[h, me, here].astype(F32)

            @pl.when(me == n - 1)
            def _():
                rising(h, me, r).wait_recv()
                out_ref[here, there] = term(h, me, r) + ru[h, me, here].astype(F32)

            @pl.when((me > 0) & (me < n - 1))
            def _():
                rising(h, me, r).wait_recv()
                falling(h, me, r).wait_recv()
                out_ref[here, there] = (
                    term(h, me, r) + ru[h, me, here].astype(F32) + rd[h, me, here].astype(F32))

    for h in range(2):
        for t in range(n - 1):
            for first, e, make, out, into in ends(t):
                @pl.when((first <= t) & (first > 0) if h == 0 else first <= t)
                def _(e=e, make=make):
                    for r in range(pieces):
                        make(h, e, r).wait_send()

    for copy in [*halo.values(), *onward.values(), *tiles.values(), *tiles_on.values()]:
        copy.wait_send()


def per_device(n, nblk, panel_vectors, force_blocks, bond_vectors, neighbours, boundary_low, boundary_high):
    rows, cols = panel_vectors.shape
    atoms = rows // 3
    half = cols // 2
    bnd = boundary_low.shape[0]
    steps = neighbours.shape[0]
    tile = nblk * cols // n
    wire = BF16 if n <= 4 else F32
    vmem = pl.BlockSpec(memory_space=pltpu.VMEM)
    hbm = pl.BlockSpec(memory_space=pltpu.HBM)
    pieces = 4 if tile % 64 == 0 else 2
    line = pltpu.VMEM((2, n, tile, half), wire)
    hops = pltpu.SemaphoreType.DMA((2 * n * pieces,))
    dma = pltpu.SemaphoreType.DMA
    shares = dma((2 * (nblk - 1),))
    result = pl.pallas_call(
        functools.partial(kernel, n, nblk, pieces),
        out_shape=pltpu.VMEM((tile, cols), F32),
        in_specs=[hbm] * 6,
        out_specs=vmem,
        scratch_shapes=[
            pltpu.VMEM((rows, cols), BF16),
            pltpu.VMEM((cols, rows), BF16),
            pltpu.VMEM((nblk, 2, half, rows), BF16),
            pltpu.VMEM((rows, rows), BF16),
            pltpu.VMEM((2, 2, half // 2, 3 * bnd), BF16),
            pltpu.VMEM((2, 2, 2, half // 2, 3 * bnd), BF16),
            pltpu.VMEM((9, steps, atoms), F32),
            pltpu.VMEM((9, steps, atoms), F32),
            pltpu.VMEM((steps, atoms), F32),
            pltpu.VMEM((steps, atoms), jnp.int32),
            pltpu.VMEM((2, 1, bnd), jnp.int32),
            pltpu.VMEM((rows + 6 * bnd, rows), BF16),
            pltpu.VMEM((rows + 6 * bnd, rows), BF16),
            pltpu.VMEM((2, half, rows), F32),
            pltpu.VMEM((2, nblk * cols, half), F32),
            line, line, line, line,
            dma((9,)), dma((4,)), dma((4,)), dma((4,)), dma((4,)),
            shares, shares, shares, shares,
            hops, hops, hops, hops,
        ],
        compiler_params=pltpu.CompilerParams(
            collective_id=0, has_side_effects=True, vmem_limit_bytes=48 * 1024 * 1024
        ),
    )(*[pltpu.with_memory_space_constraint(x, pltpu.HBM) for x in (
        panel_vectors, jnp.transpose(force_blocks, (1, 0, 2)), bond_vectors, neighbours,
        boundary_low.reshape(1, bnd), boundary_high.reshape(1, bnd))])
    scale = (3.0 * atoms * n) ** (-0.5)
    return (result * scale)[None, :, :]


def solution(mesh):
    in_specs = (
        P("dom", ("panel", "blk")),
        P(None, None, "dom"),
        P("dir", None, "dom"),
        P(None, "dom"),
        P("dom"),
        P("dom"),
    )
    out_specs = P("dir", ("panel", "dom"), "blk")
    return jax.shard_map(
        functools.partial(per_device, mesh.shape["dom"], mesh.shape["blk"]),
        mesh=mesh, in_specs=in_specs, out_specs=out_specs, check_vma=False
    )
```

```python
import functools

import jax
import jax.numpy as jnp
from jax import lax
from jax.experimental import pallas as pl
from jax.experimental.pallas import tpu as pltpu
from jax.sharding import PartitionSpec as P

MESH = pl.DeviceIdType.MESH
BF16 = jnp.bfloat16
F32 = jnp.float32


def one_hot(hits):
    return jnp.where(hits, 1.0, 0.0).astype(BF16)


def dot(a, b):
    return jnp.dot(a, b, preferred_element_type=F32)


def kernel(n, nblk, pieces, v_ref, force_ref, bond_ref, nbr_ref, low_ref, high_ref, out_ref,
           vbuf, vt, vx, perm, pick, hs, ht, fv, wq, bv, nv, lv, st_hi, st_lo, flux, part, su, ru, sd, rd,
           in_sem, h_send, h_recv, hf_send, hf_recv, x_send, x_recv, xf_send, xf_recv,
           u_send, u_recv, d_send, d_recv):
    me = lax.axis_index("dom")
    blk = lax.axis_index("blk")
    core = lax.axis_index("dir")
    rows, cols = v_ref.shape
    atoms = rows // 3
    half = cols // 2
    share = half // 2
    bnd = low_ref.shape[1]
    steps = nbr_ref.shape[0]
    tile = out_ref.shape[0]
    piece = tile // pieces
    up, down = lax.rem(me + 1, n), lax.rem(me + n - 1, n)

    def columns_of(c, h):
        return pl.ds(pl.multiple_of(h * half + c * share, share), share)

    fetches = [
        pltpu.make_async_copy(high_ref, lv.at[0], in_sem.at[0]),
        pltpu.make_async_copy(low_ref, lv.at[1], in_sem.at[1]),
        pltpu.make_async_copy(nbr_ref, nv, in_sem.at[2]),
        pltpu.make_async_copy(bond_ref.at[0], bv, in_sem.at[3]),
        pltpu.make_async_copy(force_ref, fv, in_sem.at[4]),
    ]
    by_columns = share % 128 == 0
    if by_columns:
        panel = [
            pltpu.make_async_copy(v_ref.at[:, columns_of(c, h)], vbuf.at[:, columns_of(c, h)], in_sem.at[5 + i])
            for i, (c, h) in enumerate(((core, 0), (core, 1), (1 - core, 0), (1 - core, 1)))
        ]
    else:
        panel = [pltpu.make_async_copy(v_ref, vbuf, in_sem.at[5])]
    barrier = pltpu.get_barrier_semaphore()
    peers = [{"dom": up}, {"dom": down}, {"dir": 1 - core}]
    peers += [{"blk": lax.rem(blk + o, nblk)} for o in range(1, nblk)]
    for peer in peers:
        pl.semaphore_signal(barrier, inc=1, device_id=peer, device_id_type=MESH)
    for copy in [*fetches[:2], *panel, *fetches[2:]]:
        copy.start()

    row_of = lax.broadcasted_iota(jnp.int32, (rows, atoms), 0)
    atom_of = lax.broadcasted_iota(jnp.int32, (rows, atoms), 1)
    for a in range(3):
        perm[:, a * atoms:(a + 1) * atoms] = one_hot(row_of == 3 * atom_of + a)
    fetches[0].wait()
    fetches[1].wait()
    natural = lax.broadcasted_iota(jnp.int32, (rows, bnd), 0)
    for side in range(2):
        for b in range(3):
            pick[:, (3 * side + b) * bnd:(3 * side + b + 1) * bnd] = one_hot(natural == 3 * lv[side] + b)

    def turn_columns(c):
        if by_columns:
            turned = [vbuf[:, columns_of(c, h)].T for h in range(2)]
        else:
            turned = [vt[columns_of(c, h), :] for h in range(2)]
        return jnp.concatenate(turned, axis=0)

    def sort_rows(c, turned):
        sorted_rows = dot(turned, perm[...]).astype(BF16)
        for h in range(2):
            vx[blk, h, pl.ds(pl.multiple_of(c * share, share), share), :] = sorted_rows[h * share:(h + 1) * share]

    for copy in panel[:2]:
        copy.wait()
    if not by_columns:
        vt[...] = vbuf[...].T
    mine = turn_columns(core)
    rows_out = dot(mine, pick[...]).astype(BF16)
    for side in range(2):
        for h in range(2):
            hs[side, h] = rows_out[h * share:(h + 1) * share, 3 * side * bnd:3 * (side + 1) * bnd]
    pl.semaphore_wait(barrier, len(peers))

    halo = {
        (side, h): pltpu.make_async_remote_copy(
            src_ref=hs.at[side, h], dst_ref=ht.at[side, h, core],
            send_sem=h_send.at[2 * side + h], recv_sem=h_recv.at[2 * side + h],
            device_id={"dom": up if side == 0 else down}, device_id_type=MESH)
        for h in range(2) for side in range(2)
    }
    for side in range(2):
        halo[side, 0].start()
    sort_rows(core, mine)

    my_share = pl.ds(pl.multiple_of(core * share, share), share)

    def x_half(b, p):
        return lax.rem(b + p, 2)

    tiles = {
        (o, p): pltpu.make_async_remote_copy(
            src_ref=vx.at[blk, x_half(blk, p), my_share], dst_ref=vx.at[blk, x_half(blk, p), my_share],
            send_sem=x_send.at[2 * (o - 1) + p], recv_sem=x_recv.at[2 * (o - 1) + p],
            device_id={"blk": lax.rem(blk + o, nblk)}, device_id_type=MESH)
        for o in range(1, nblk) for p in range(2)
    }
    for o in range(1, nblk):
        tiles[o, 0].start()
    for copy in panel[2:]:
        copy.wait()
    sort_rows(1 - core, turn_columns(1 - core))

    for copy in fetches[2:]:
        copy.wait()
    for q in range(9):
        wq[q] = fv[q] * bv[...]
    names = nv[...]
    k_of = lax.broadcasted_iota(jnp.int32, names.shape, 0)
    totals = [wq[q] for q in range(9)]
    for s in range(1, steps):
        same = (names == pltpu.roll(names, s, 0)) & (k_of >= s)
        for q in range(9):
            totals[q] = totals[q] + jnp.where(same, pltpu.roll(wq[q], s, 0), 0.0)
    for q in range(9):
        wq[q] = totals[q]

    sub, lanes, group = 8, 128, 32

    def build(first, count, base, stride):
        def body(t, carry):
            j0 = pl.multiple_of(t * group, group)
            for i0 in range(0, atoms, lanes):
                here = slice(i0, i0 + lanes)
                strips = range(group // sub)
                js = [lax.broadcasted_iota(jnp.int32, (sub, lanes), 0) + (j0 + first + s * sub) for s in strips]
                found = [jnp.full((sub, lanes), -1, jnp.int32) for _ in strips]
                for k in range(steps):
                    name = jnp.broadcast_to(nv[k:k + 1, here], (sub, lanes))
                    for s in strips:
                        found[s] = jnp.where(js[s] == name, k, found[s])
                spot = [f & (sub - 1) for f in found]
                for a in range(3):
                    for b in range(3):
                        values = []
                        for s in strips:
                            value = jnp.zeros((sub, lanes), F32)
                            for k0 in range(0, steps, sub):
                                taken = jnp.take_along_axis(
                                    wq[3 * a + b, k0:k0 + sub, here], spot[s], axis=0, mode="promise_in_bounds")
                                value = jnp.where(found[s] >= k0, taken, value)
                            values.append(value)
                        value = jnp.concatenate(values, axis=0)
                        high = value.astype(BF16)
                        at = (pl.ds(pl.multiple_of(base + b * stride + j0, group), group),
                              slice(a * atoms + i0, a * atoms + i0 + lanes))
                        st_hi[at] = high
                        st_lo[at] = (value - high.astype(F32)).astype(BF16)
            return carry

        lax.fori_loop(0, count // group, body, 0)

    build(0, atoms, 0, atoms)
    for o in range(1, nblk):
        tiles[o, 1].start()
    build(atoms, bnd, rows, bnd)
    build(atoms + bnd, bnd, rows + 3 * bnd, bnd)
    for side in range(2):
        halo[side, 1].start()

    onward = {}
    tiles_on = {}

    def pass_halo(h):
        for side in range(2):
            halo[side, h].wait_recv()
            onward[side, h] = pltpu.make_async_remote_copy(
                src_ref=ht.at[side, h, core], dst_ref=ht.at[side, h, core],
                send_sem=hf_send.at[2 * side + h], recv_sem=hf_recv.at[2 * side + h],
                device_id={"dir": 1 - core}, device_id_type=MESH)
            onward[side, h].start()

    def source(o):
        return lax.rem(blk + nblk - o, nblk)

    def pass_tiles(p):
        for o in range(1, nblk):
            tiles[o, p].wait_recv()
            spot = (source(o), x_half(source(o), p), my_share)
            tiles_on[o, p] = pltpu.make_async_remote_copy(
                src_ref=vx.at[spot], dst_ref=vx.at[spot],
                send_sem=xf_send.at[2 * (o - 1) + p], recv_sem=xf_recv.at[2 * (o - 1) + p],
                device_id={"dir": 1 - core}, device_id_type=MESH)
            tiles_on[o, p].start()

    def term(h, e, r):
        return part[h, pl.ds(pl.multiple_of(e * tile + r * piece, piece), piece), :]

    def hop(h, e, r, out, into, send, recv, target):
        cell = (h * n + e) * pieces + r
        here = pl.ds(r * piece, piece)
        return pltpu.make_async_remote_copy(
            src_ref=out.at[h, e, here], dst_ref=into.at[h, e, here],
            send_sem=send.at[cell], recv_sem=recv.at[cell],
            device_id={"dom": target}, device_id_type=MESH)

    def rising(h, e, r):
        return hop(h, e, r, su, ru, u_send, u_recv, up)

    def falling(h, e, r):
        return hop(h, e, r, sd, rd, d_send, d_recv, down)

    def ends(t):
        return ((me, n - 1 - (t - me), rising, su, ru),
                (n - 1 - me, t - (n - 1 - me), falling, sd, rd))

    def own_flux(h):
        own = vx[blk, h]
        flux[h] = dot(own, st_hi[:rows, :]) + dot(own, st_lo[:rows, :])

    def couple(h):
        for side in range(2):
            onward[side, h].wait_recv()
        outer = jnp.concatenate(
            [jnp.concatenate([ht[side, h, c] for side in range(2)], axis=1) for c in range(2)], axis=0)
        total = flux[h] + dot(outer, st_hi[rows:, :]) + dot(outer, st_lo[rows:, :])
        return total.astype(BF16).T

    def multiply(h, b, u, columns):
        part[h, pl.ds(pl.multiple_of((2 * b + u) * half, half), half), :] = dot(vx[b, u], columns)

    far, near = (blk == nblk - 1, blk == 0), (blk < nblk - 1, blk > 0)
    always = (True, True)
    if n == 4 and nblk == 2:
        first_part, second_part, third_part = [(0, far), (1, far), (2, near)], [(0, near)], [(2, far), (1, near)]
    else:
        first_part, second_part, third_part = [], [], [(t, always) for t in range(n - 1)]

    def emit(t, h, where):
        for (first, e, make, out, into), here in zip(ends(t), where):
            @pl.when((first == 0) & here)
            def _(e=e, make=make, out=out):
                if h == 1:
                    for r in range(pieces):
                        make(0, e, r).wait_send()
                for r in range(pieces):
                    out[h, e, r * piece:(r + 1) * piece] = term(h, e, r).astype(out.dtype)
                    make(h, e, r).start()

    def forward(h):
        for t in range(1, n - 1):
            for r in range(pieces):
                for first, e, make, out, into in ends(t):
                    @pl.when((first > 0) & (first <= t))
                    def _(r=r, e=e, make=make, out=out, into=into):
                        here = slice(r * piece, (r + 1) * piece)
                        make(h, e, r).wait_recv()
                        out[h, e, here] = (term(h, e, r) + into[h, e, here].astype(F32)).astype(out.dtype)
                        make(h, e, r).start()

    own_flux(0)
    own_flux(1)
    pass_halo(0)
    columns = couple(0)
    for u in range(2):
        multiply(0, blk, u, columns)
    for t, where in first_part:
        emit(t, 0, where)
    pass_tiles(0)
    for o in range(1, nblk):
        tiles_on[o, 0].wait_recv()
        multiply(0, source(o), x_half(source(o), 0), columns)
    for t, where in second_part:
        emit(t, 0, where)
    pass_tiles(1)
    pass_halo(1)
    for o in range(1, nblk):
        tiles_on[o, 1].wait_recv()
        multiply(0, source(o), x_half(source(o), 1), columns)
    for t, where in third_part:
        emit(t, 0, where)
    later = couple(1)
    forward(0)
    for u in range(2):
        multiply(1, blk, u, later)
    for o in range(1, nblk):
        for p in range(2):
            multiply(1, source(o), x_half(source(o), p), later)
    for t in range(n - 1):
        emit(t, 1, always)
    forward(1)

    for h in range(2):
        for r in range(pieces):
            here = slice(r * piece, (r + 1) * piece)
            there = slice(h * half, (h + 1) * half)

            @pl.when(me == 0)
            def _():
                falling(h, me, r).wait_recv()
                out_ref[here, there] = term(h, me, r) + rd[h, me, here].astype(F32)

            @pl.when(me == n - 1)
            def _():
                rising(h, me, r).wait_recv()
                out_ref[here, there] = term(h, me, r) + ru[h, me, here].astype(F32)

            @pl.when((me > 0) & (me < n - 1))
            def _():
                rising(h, me, r).wait_recv()
                falling(h, me, r).wait_recv()
                out_ref[here, there] = (
                    term(h, me, r) + ru[h, me, here].astype(F32) + rd[h, me, here].astype(F32))

    for h in range(2):
        for t in range(n - 1):
            for first, e, make, out, into in ends(t):
                @pl.when((first <= t) & (first > 0) if h == 0 else first <= t)
                def _(e=e, make=make):
                    for r in range(pieces):
                        make(h, e, r).wait_send()

    for copy in [*halo.values(), *onward.values(), *tiles.values(), *tiles_on.values()]:
        copy.wait_send()


def per_device(n, nblk, panel_vectors, force_blocks, bond_vectors, neighbours, boundary_low, boundary_high):
    rows, cols = panel_vectors.shape
    atoms = rows // 3
    half = cols // 2
    bnd = boundary_low.shape[0]
    steps = neighbours.shape[0]
    tile = nblk * cols // n
    wire = BF16 if n <= 4 else F32
    vmem = pl.BlockSpec(memory_space=pltpu.VMEM)
    hbm = pl.BlockSpec(memory_space=pltpu.HBM)
    pieces = 4 if tile % 64 == 0 else 2
    line = pltpu.VMEM((2, n, tile, half), wire)
    hops = pltpu.SemaphoreType.DMA((2 * n * pieces,))
    dma = pltpu.SemaphoreType.DMA
    shares = dma((2 * (nblk - 1),))
    result = pl.pallas_call(
        functools.partial(kernel, n, nblk, pieces),
        out_shape=pltpu.VMEM((tile, cols), F32),
        in_specs=[hbm] * 6,
        out_specs=vmem,
        scratch_shapes=[
            pltpu.VMEM((rows, cols), BF16),
            pltpu.VMEM((cols, rows), BF16),
            pltpu.VMEM((nblk, 2, half, rows), BF16),
            pltpu.VMEM((rows, rows), BF16),
            pltpu.VMEM((rows, 6 * bnd), BF16),
            pltpu.VMEM((2, 2, half // 2, 3 * bnd), BF16),
            pltpu.VMEM((2, 2, 2, half // 2, 3 * bnd), BF16),
            pltpu.VMEM((9, steps, atoms), F32),
            pltpu.VMEM((9, steps, atoms), F32),
            pltpu.VMEM((steps, atoms), F32),
            pltpu.VMEM((steps, atoms), jnp.int32),
            pltpu.VMEM((2, 1, bnd), jnp.int32),
            pltpu.VMEM((rows + 6 * bnd, rows), BF16),
            pltpu.VMEM((rows + 6 * bnd, rows), BF16),
            pltpu.VMEM((2, half, rows), F32),
            pltpu.VMEM((2, nblk * cols, half), F32),
            line, line, line, line,
            dma((9,)), dma((4,)), dma((4,)), dma((4,)), dma((4,)),
            shares, shares, shares, shares,
            hops, hops, hops, hops,
        ],
        compiler_params=pltpu.CompilerParams(
            collective_id=0, has_side_effects=True, vmem_limit_bytes=48 * 1024 * 1024
        ),
    )(*[pltpu.with_memory_space_constraint(x, pltpu.HBM) for x in (
        panel_vectors, jnp.transpose(force_blocks, (1, 0, 2)), bond_vectors, neighbours,
        boundary_low.reshape(1, bnd), boundary_high.reshape(1, bnd))])
    scale = (3.0 * atoms * n) ** (-0.5)
    return (result * scale)[None, :, :]


def solution(mesh):
    in_specs = (
        P("dom", ("panel", "blk")),
        P(None, None, "dom"),
        P("dir", None, "dom"),
        P(None, "dom"),
        P("dom"),
        P("dom"),
    )
    out_specs = P("dir", ("panel", "dom"), "blk")
    return jax.shard_map(
        functools.partial(per_device, mesh.shape["dom"], mesh.shape["blk"]),
        mesh=mesh, in_specs=in_specs, out_specs=out_specs, check_vma=False
    )
```
